128 devices in a mesh: col: 32 (over y, x, core), row: 4 (over z).
Axes of the slice: x: 4, y: 4, z: 4, core: 2. Of those that a mesh axis runs over, the one named last changes fastest.
Arguments:
- sources_field: float32 [2, 31744, 128], P(None, ('col', 'row')), may hold values from -6 to 6
- data: float32 [2, 52224, 128], P(None, ('col', 'row')), may hold values from -6 to 6
- left_basis: float32 [2, 32, 52224, 128], P(None, None, ('col', 'row')), may hold values from -0.09375 to 0.09375
- right_basis: float32 [2, 32, 31744, 128], P(None, None, ('col', 'row')), may hold values from -0.1875 to 0.1875
- ranks: int32 [32, 32], replicated, may hold values from 32 to 128, as said below
Outputs:
- residual: float32 [2, 52224, 128], P(None, ('col', 'row'))
- gradient: float32 [2, 31744, 128], P(None, ('col', 'row'))
The draws below stay inside these ranges and needn't reach their ends.
Inputs may be any that keep to these rules, and one draw needn't show every extreme that they name: `ranks`: every rank is a multiple of 32.
All inputs are finite; a program needn't handle non-finite values.
Results may differ from the reference program's by a relative error of at most 0.000059.
Values sent between devices are 32-bit elements; how exact they have to be, the bound alone decides.
A program may use at most 128 MiB of HBM per device.

```python
import jax
import jax.numpy as jnp
from jax import lax

MB = 1632
NB = 992
KMAX = 128
S = 128
TILES = 32
NROWS = 52224
NCOLS = 31744


def draw_ranks(key, part):
    levels = jax.random.randint(jax.random.fold_in(key, 17), (TILES, TILES), 1, 5)
    levels = levels.at[0, 0].set(4).at[0, 1].set(1)
    return (levels * (KMAX // 4)).astype(jnp.int32)


def steps_of(key, extent, split, low, top_value):
    def one(axis_at, shards_of):
        steps = jax.random.uniform(jax.random.fold_in(jax.random.fold_in(key, 6), axis_at), (shards_of,), jnp.float32, low / len(split), top_value / len(split))
        return jnp.repeat(jnp.exp(steps), extent[axis_at] // shards_of).reshape((-1,) + (1,) * (len(extent) - axis_at - 1))

    gain = one(*split[0])
    for cut in split[1:]:
        gain = gain * one(*cut)
    return gain


def bell_draw(key, shape, scale, limit, cuts=(), kind=jnp.bfloat16):
    array = jax.random.normal(key, shape, jnp.float32) * scale
    if len(cuts) > 0:
        array = steps_of(key, shape, cuts, -0.22, 0.18) * array
    return jnp.clip(array, min=-limit, max=limit).astype(kind)


def setup_inputs(seed: int = 0) -> dict:
    keys = jax.random.split(jax.random.key(seed), 6)
    return {
        "sources_field": bell_draw(keys[0], (2, NCOLS, S), 1.0, 6.0, ((1, 128),), jnp.float32),
        "data": bell_draw(keys[1], (2, NROWS, S), 1.0, 6.0, ((1, 128),), jnp.float32),
        "left_basis": bell_draw(keys[2], (2, TILES, NROWS, KMAX), (KMAX * TILES) ** -0.5, 0.09375, ((2, 128),), jnp.float32),
        "right_basis": bell_draw(keys[3], (2, TILES, NCOLS, KMAX), NB ** -0.5, 0.1875, ((2, 128),), jnp.float32),
        "ranks": draw_ranks(jax.random.fold_in(keys[5], 71), 0),
    }


def contract(form, left, right):
    return jnp.einsum(form, left, right, precision=lax.Precision.HIGHEST, preferred_element_type=jnp.float32)


def reference(sources_field, data, left_basis, right_basis, ranks):
    xr = sources_field[0].reshape(TILES, NB, S)
    xi = sources_field[1].reshape(TILES, NB, S)
    vr = right_basis[0].reshape(TILES, TILES, NB, KMAX)
    vi = right_basis[1].reshape(TILES, TILES, NB, KMAX)
    ur = left_basis[0].reshape(TILES, TILES, MB, KMAX)
    ui = left_basis[1].reshape(TILES, TILES, MB, KMAX)
    levels = jnp.arange(KMAX, dtype=jnp.int32)
    keep = (levels[None, None, :] < ranks[:, :, None]).astype(jnp.float32)[..., None]
    zr = (contract('ijnk,jns->ijks', vr, xr) + contract('ijnk,jns->ijks', vi, xi)) * keep
    zi = (contract('ijnk,jns->ijks', vr, xi) - contract('ijnk,jns->ijks', vi, xr)) * keep
    yr = contract('jimk,ijks->ims', ur, zr) - contract('jimk,ijks->ims', ui, zi)
    yi = contract('jimk,ijks->ims', ur, zi) + contract('jimk,ijks->ims', ui, zr)
    predicted = jnp.stack([yr.reshape(NROWS, S), yi.reshape(NROWS, S)])
    residual = predicted - data
    rr = residual[0].reshape(TILES, MB, S)
    ri = residual[1].reshape(TILES, MB, S)
    wr = (contract('jimk,ims->ijks', ur, rr) + contract('jimk,ims->ijks', ui, ri)) * keep
    wi = (contract('jimk,ims->ijks', ur, ri) - contract('jimk,ims->ijks', ui, rr)) * keep
    gr = contract('ijnk,ijks->jns', vr, wr) - contract('ijnk,ijks->jns', vi, wi)
    gi = contract('ijnk,ijks->jns', vr, wi) + contract('ijnk,ijks->jns', vi, wr)
    gradient = jnp.stack([gr.reshape(NCOLS, S), gi.reshape(NCOLS, S)])
    return residual, gradient
```

```python
import functools

import jax
import jax.numpy as jnp
from jax import lax
from jax.experimental import pallas as pl
from jax.experimental.pallas import tpu as pltpu
from jax.sharding import PartitionSpec as P

MESH = pl.DeviceIdType.MESH
F32 = jnp.float32
BF16 = jnp.bfloat16
GROUP = 4


def halves(a):
    hi = a.astype(BF16)
    return hi, (a - hi.astype(F32)).astype(BF16)


def dot3(a, b, contract):
    def dot(x, y):
        return lax.dot_general(x, y, (contract, ((), ())), preferred_element_type=F32)

    (ah, al), (bh, bl) = a, b
    return dot(ah, bh) + (dot(ah, bl) + dot(al, bh))


def kernel(
    tiles, group, ranks, x_any, d_any, u_any, v_any, res_any, grad_any,
    x, d, u, v, part, r1, r2, z, xt, rt, acc_u, acc_v, grad,
    x_sem, d_sem, v_sem, u_sem, out_sem, self_sem,
    rs1_send, rs2_send, a2a_send, ag1_send, ag2_send,
    rs1_recv, rs2_recv, a2a_recv, ag1_recv, ag2_recv,
):
    c = lax.axis_index("col")
    r = lax.axis_index("row")
    s = part.shape[-2]
    quarter = s // 4
    groups = tiles // group
    right, left = (c, lax.rem(r + 1, 4)), (c, lax.rem(r + 3, 4))

    barrier = pltpu.get_barrier_semaphore()

    def greet(t, _):
        peer = (lax.rem(c + t, tiles), r)
        pl.semaphore_signal(barrier, inc=1, device_id=peer, device_id_type=MESH)
        return 0

    lax.fori_loop(1, tiles, greet, 0)
    pl.semaphore_signal(barrier, inc=1, device_id=right, device_id_type=MESH)
    pl.semaphore_signal(barrier, inc=1, device_id=left, device_id_type=MESH)

    copy_x = pltpu.make_async_copy(x_any, x, x_sem)
    copy_x.start()

    def fetch_v(t, _):
        pltpu.make_async_copy(
            v_any.at[:, lax.rem(c + t, tiles)], v.at[:, t], v_sem.at[t // group]
        ).start()
        return 0

    lax.fori_loop(0, tiles, fetch_v, 0)

    def fetch_u(t, _):
        pltpu.make_async_copy(u_any.at[:, lax.rem(c + t, tiles)], u.at[:, t], u_sem).start()
        return 0

    lax.fori_loop(0, tiles, fetch_u, 0)
    copy_d = pltpu.make_async_copy(d_any, d, d_sem)
    copy_d.start()

    def rows(q):
        return pl.ds(pl.multiple_of(q * quarter, quarter), quarter)

    def span(g):
        return pl.ds(g * group, group)

    def turned(values, dst):
        for p in range(2):
            hi, lo = halves(values[p].T)
            dst[0, p * s : (p + 1) * s] = hi
            dst[1, p * s : (p + 1) * s] = lo

    def wait_for(ref, sem):
        pltpu.make_async_copy(ref, ref, sem).wait()

    def phase(ph, made_from, lhs, rank_of, spread_by, acc):
        q_right, q_left, q_far = lax.rem(r + 1, 4), lax.rem(r + 3, 4), lax.rem(r + 2, 4)

        def send(src, dst, send_sem, recv_sem, to):
            pltpu.make_async_remote_copy(
                src_ref=src, dst_ref=dst, send_sem=send_sem, recv_sem=recv_sem,
                device_id=to, device_id_type=MESH,
            ).start()

        def produce(g):
            if ph == 0:
                wait_for(v.at[:, span(g)], v_sem.at[g])

            def one(k, _):
                t = g * group + k
                both = jnp.concatenate([made_from[0, t], made_from[1, t]], axis=1)
                y = dot3((lhs[0], lhs[1]), halves(both), ((1,), (0,)))
                kmax = y.shape[1] // 2
                level = lax.broadcasted_iota(jnp.int32, (s, kmax), 1)
                keep = level < rank_of(t)
                part[0, t] = jnp.where(keep, y[:s, :kmax] + y[s:, kmax:], 0.0)
                part[1, t] = jnp.where(keep, y[s:, :kmax] - y[:s, kmax:], 0.0)
                return 0

            lax.fori_loop(0, group, one, 0)

        def rs1(g):
            send(part.at[0, span(g), rows(q_far)], r1.at[ph, 0, span(g)],
                 rs1_send.at[ph, 0], rs1_recv.at[ph, 0, g], right)
            send(part.at[1, span(g), rows(q_far)], r1.at[ph, 1, span(g)],
                 rs1_send.at[ph, 1], rs1_recv.at[ph, 1, g], left)

        def rs2(g):
            for h, q, to in ((0, q_right, right), (1, q_left, left)):
                wait_for(r1.at[ph, h, span(g)], rs1_recv.at[ph, h, g])
                part[h, span(g), rows(q)] = part[h, span(g), rows(q)] + r1[ph, h, span(g)]
                send(part.at[:, span(g), rows(q)], r2.at[ph, h, :, span(g)],
                     rs2_send.at[ph, h], rs2_recv.at[ph, h, g], to)

        def settle(g):
            for h in range(2):
                wait_for(r2.at[ph, h, :, span(g)], rs2_recv.at[ph, h, g])
            for h in range(2):
                part[h, span(g), rows(r)] = part[h, span(g), rows(r)] + (
                    r2[ph, 0, h, span(g)] + r2[ph, 1, h, span(g)]
                )

            def one(k, _):
                t = g * group + k
                src, dst = part.at[:, t, rows(r)], z.at[ph, :, t, rows(r)]

                @pl.when(t == 0)
                def _():
                    pltpu.make_async_copy(src, dst, self_sem.at[ph]).start()

                @pl.when(t > 0)
                def _():
                    send(src, dst, a2a_send.at[ph], a2a_recv.at[ph, g], (lax.rem(c + t, tiles), r))

                return 0

            lax.fori_loop(0, group, one, 0)

        def ag1(g):
            @pl.when(g == 0)
            def _():
                wait_for(z.at[ph, :, 0, rows(r)], self_sem.at[ph])
                if group > 1:
                    wait_for(z.at[ph, :, pl.ds(1, group - 1), rows(r)], a2a_recv.at[ph, 0])

            @pl.when(g > 0)
            def _():
                wait_for(z.at[ph, :, span(g), rows(r)], a2a_recv.at[ph, g])

            own = z.at[ph, :, span(g), rows(r)]
            send(own, own, ag1_send.at[ph, 0], ag1_recv.at[ph, 0, g], right)
            send(own, own, ag1_send.at[ph, 1], ag1_recv.at[ph, 1, g], left)

        def ag2(g):
            for h, q, to in ((0, q_left, right), (1, q_right, left)):
                wait_for(z.at[ph, :, span(g), rows(q)], ag1_recv.at[ph, h, g])
                passed = z.at[ph, h, span(g), rows(q)]
                send(passed, passed, ag2_send.at[ph, h], ag2_recv.at[ph, h, g], to)

        def consume(g):
            for h in range(2):
                wait_for(z.at[ph, h, span(g), rows(q_far)], ag2_recv.at[ph, h, g])

            def one(k, _):
                t = g * group + k
                slot = lax.rem(tiles - t, tiles)
                both = jnp.concatenate([spread_by[0, slot], spread_by[1, slot]], axis=1)
                (ah, al), (bh, bl) = halves(z[ph, 0, t]), halves(z[ph, 1, t])

                def square(a, b):
                    return jnp.concatenate(
                        [jnp.concatenate([a, -b], axis=1), jnp.concatenate([b, a], axis=1)], axis=0
                    )

                acc[...] += dot3(halves(both), (square(ah, bh), square(al, bl)), ((1,), (1,)))
                return 0

            lax.fori_loop(0, group, one, 0)

        def step(it, _):
            def at(lag, f):
                g = it - lag

                @pl.when((g >= 0) & (g < groups))
                def _():
                    f(g)

            at(0, produce)
            at(0, rs1)
            at(lag, ag1)
            at(1, rs2)
            at(2, settle)
            at(lag + 1, ag2)
            if ph == 0:

                @pl.when(it == lag + 2)
                def _():
                    wait_for(u, u_sem)

            at(lag + 2, consume)
            return 0

        lag = max(groups - 2, 3)
        if ph == 0:
            copy_x.wait()
            turned(x, xt)
        acc[...] = jnp.zeros_like(acc)
        if ph == 0:
            pl.semaphore_wait(barrier, tiles + 1)
        lax.fori_loop(0, groups + lag + 2, step, 0)

        for h, q_sum, q_pass in ((0, q_right, q_left), (1, q_left, q_right)):
            wait_for(part.at[h, :, rows(q_far)], rs1_send.at[ph, h])
            wait_for(part.at[:, :, rows(q_sum)], rs2_send.at[ph, h])
            wait_for(z.at[ph, :, :, rows(r)], ag1_send.at[ph, h])
            wait_for(z.at[ph, h, :, rows(q_pass)], ag2_send.at[ph, h])
        wait_for(part.at[:, pl.ds(1, tiles - 1), rows(r)], a2a_send.at[ph])

    phase(0, v, xt, lambda t: ranks[lax.rem(c + t, tiles), c], u, acc_u)
    copy_d.wait()
    for p in range(2):
        d[p] = acc_u[:, p * s : (p + 1) * s] - d[p]
    turned(d, rt)
    copy_res = pltpu.make_async_copy(d, res_any, out_sem.at[0])
    copy_res.start()
    phase(1, u, rt, lambda t: ranks[c, lax.rem(c + t, tiles)], v, acc_v)
    for p in range(2):
        grad[p] = acc_v[:, p * s : (p + 1) * s]
    copy_grad = pltpu.make_async_copy(grad, grad_any, out_sem.at[1])
    copy_grad.start()
    copy_res.wait()
    copy_grad.wait()


def on_device(tiles, group, sources_field, data, left_basis, right_basis, ranks):
    _, n, s = sources_field.shape
    m = data.shape[1]
    k = left_basis.shape[-1]
    groups = tiles // group
    dma = pltpu.SemaphoreType.DMA
    whole = pl.BlockSpec(memory_space=pl.ANY)
    return pl.pallas_call(
        functools.partial(kernel, tiles, group),
        out_shape=(
            jax.ShapeDtypeStruct((2, m, s), F32),
            jax.ShapeDtypeStruct((2, n, s), F32),
        ),
        in_specs=[pl.BlockSpec(memory_space=pltpu.SMEM)] + [whole] * 4,
        out_specs=(whole, whole),
        scratch_shapes=[
            pltpu.VMEM((2, n, s), F32),
            pltpu.VMEM((2, m, s), F32),
            pltpu.VMEM((2, tiles, m, k), F32),
            pltpu.VMEM((2, tiles, n, k), F32),
            pltpu.VMEM((2, tiles, s, k), F32),
            pltpu.VMEM((2, 2, tiles, s // 4, k), F32),
            pltpu.VMEM((2, 2, 2, tiles, s // 4, k), F32),
            pltpu.VMEM((2, 2, tiles, s, k), F32),
            pltpu.VMEM((2, 2 * s, n), BF16),
            pltpu.VMEM((2, 2 * s, m), BF16),
            pltpu.VMEM((m, 2 * s), F32),
            pltpu.VMEM((n, 2 * s), F32),
            pltpu.VMEM((2, n, s), F32),
            dma, dma, dma((groups,)), dma, dma((2,)), dma((2,)),
            dma((2, 2)), dma((2, 2)), dma((2,)), dma((2, 2)), dma((2, 2)),
            dma((2, 2, groups)), dma((2, 2, groups)), dma((2, groups)),
            dma((2, 2, groups)), dma((2, 2, groups)),
        ],
        compiler_params=pltpu.CompilerParams(
            collective_id=0, has_side_effects=True, vmem_limit_bytes=60 * 1024 * 1024
        ),
        name="tlr_step",
    )(ranks, sources_field, data, left_basis, right_basis)


def solution(mesh):
    tiles = mesh.shape["col"]
    group = GROUP if tiles % GROUP == 0 and tiles > 2 * GROUP else 1
    placed = P(None, ("col", "row"), None)
    bases = P(None, None, ("col", "row"), None)
    return jax.shard_map(
        functools.partial(on_device, tiles, group),
        mesh=mesh,
        in_specs=(placed, placed, bases, bases, P()),
        out_specs=(placed, placed),
        check_vma=False,
    )
```

```python
import functools

import jax
import jax.numpy as jnp
from jax import lax
from jax.experimental import pallas as pl
from jax.experimental.pallas import tpu as pltpu
from jax.sharding import PartitionSpec as P

MESH = pl.DeviceIdType.MESH
F32 = jnp.float32
BF16 = jnp.bfloat16
GROUP = 4
PACKS = 25
PACK_GROUP = 5


def halves(a):
    hi = a.astype(BF16)
    return hi, (a - hi.astype(F32)).astype(BF16)


def dot3(a, b, contract):
    def dot(x, y):
        return lax.dot_general(x, y, (contract, ((), ())), preferred_element_type=F32)

    (ah, al), (bh, bl) = a, b
    return dot(ah, bh) + (dot(ah, bl) + dot(al, bh))


def plain_kernel(
    tiles, group, ranks, x_any, d_any, u_any, v_any, res_any, grad_any,
    x, d, u, v, part, r1, r2, z, xt, rt, acc_u, acc_v, grad,
    x_sem, d_sem, v_sem, u_sem, out_sem, self_sem,
    rs1_send, rs2_send, a2a_send, ag1_send, ag2_send,
    rs1_recv, rs2_recv, a2a_recv, ag1_recv, ag2_recv,
):
    c = lax.axis_index("col")
    r = lax.axis_index("row")
    s = part.shape[-2]
    quarter = s // 4
    groups = tiles // group
    right, left = (c, lax.rem(r + 1, 4)), (c, lax.rem(r + 3, 4))

    barrier = pltpu.get_barrier_semaphore()

    def greet(t, _):
        peer = (lax.rem(c + t, tiles), r)
        pl.semaphore_signal(barrier, inc=1, device_id=peer, device_id_type=MESH)
        return 0

    lax.fori_loop(1, tiles, greet, 0)
    pl.semaphore_signal(barrier, inc=1, device_id=right, device_id_type=MESH)
    pl.semaphore_signal(barrier, inc=1, device_id=left, device_id_type=MESH)

    copy_x = pltpu.make_async_copy(x_any, x, x_sem)
    copy_x.start()

    def fetch_v(t, _):
        pltpu.make_async_copy(
            v_any.at[:, lax.rem(c + t, tiles)], v.at[:, t], v_sem.at[t // group]
        ).start()
        return 0

    lax.fori_loop(0, tiles, fetch_v, 0)

    def fetch_u(t, _):
        pltpu.make_async_copy(u_any.at[:, lax.rem(c + t, tiles)], u.at[:, t], u_sem).start()
        return 0

    lax.fori_loop(0, tiles, fetch_u, 0)
    copy_d = pltpu.make_async_copy(d_any, d, d_sem)
    copy_d.start()

    def rows(q):
        return pl.ds(pl.multiple_of(q * quarter, quarter), quarter)

    def span(g):
        return pl.ds(g * group, group)

    def turned(values, dst):
        for p in range(2):
            hi, lo = halves(values[p].T)
            dst[0, p * s : (p + 1) * s] = hi
            dst[1, p * s : (p + 1) * s] = lo

    def wait_for(ref, sem):
        pltpu.make_async_copy(ref, ref, sem).wait()

    def phase(ph, made_from, lhs, rank_of, spread_by, acc):
        q_right, q_left, q_far = lax.rem(r + 1, 4), lax.rem(r + 3, 4), lax.rem(r + 2, 4)

        def send(src, dst, send_sem, recv_sem, to):
            pltpu.make_async_remote_copy(
                src_ref=src, dst_ref=dst, send_sem=send_sem, recv_sem=recv_sem,
                device_id=to, device_id_type=MESH,
            ).start()

        def produce(g):
            if ph == 0:
                wait_for(v.at[:, span(g)], v_sem.at[g])

            def one(k, _):
                t = g * group + k
                both = jnp.concatenate([made_from[0, t], made_from[1, t]], axis=1)
                y = dot3((lhs[0], lhs[1]), halves(both), ((1,), (0,)))
                kmax = y.shape[1] // 2
                level = lax.broadcasted_iota(jnp.int32, (s, kmax), 1)
                keep = level < rank_of(t)
                part[0, t] = jnp.where(keep, y[:s, :kmax] + y[s:, kmax:], 0.0)
                part[1, t] = jnp.where(keep, y[s:, :kmax] - y[:s, kmax:], 0.0)
                return 0

            lax.fori_loop(0, group, one, 0)

        def rs1(g):
            send(part.at[0, span(g), rows(q_far)], r1.at[ph, 0, span(g)],
                 rs1_send.at[ph, 0], rs1_recv.at[ph, 0, g], right)
            send(part.at[1, span(g), rows(q_far)], r1.at[ph, 1, span(g)],
                 rs1_send.at[ph, 1], rs1_recv.at[ph, 1, g], left)

        def rs2(g):
            for h, q, to in ((0, q_right, right), (1, q_left, left)):
                wait_for(r1.at[ph, h, span(g)], rs1_recv.at[ph, h, g])
                part[h, span(g), rows(q)] = part[h, span(g), rows(q)] + r1[ph, h, span(g)]
                send(part.at[:, span(g), rows(q)], r2.at[ph, h, :, span(g)],
                     rs2_send.at[ph, h], rs2_recv.at[ph, h, g], to)

        def settle(g):
            for h in range(2):
                wait_for(r2.at[ph, h, :, span(g)], rs2_recv.at[ph, h, g])
            for h in range(2):
                part[h, span(g), rows(r)] = part[h, span(g), rows(r)] + (
                    r2[ph, 0, h, span(g)] + r2[ph, 1, h, span(g)]
                )

            def one(k, _):
                t = g * group + k
                src, dst = part.at[:, t, rows(r)], z.at[ph, :, t, rows(r)]

                @pl.when(t == 0)
                def _():
                    pltpu.make_async_copy(src, dst, self_sem.at[ph]).start()

                @pl.when(t > 0)
                def _():
                    send(src, dst, a2a_send.at[ph], a2a_recv.at[ph, g], (lax.rem(c + t, tiles), r))

                return 0

            lax.fori_loop(0, group, one, 0)

        def ag1(g):
            @pl.when(g == 0)
            def _():
                wait_for(z.at[ph, :, 0, rows(r)], self_sem.at[ph])
                if group > 1:
                    wait_for(z.at[ph, :, pl.ds(1, group - 1), rows(r)], a2a_recv.at[ph, 0])

            @pl.when(g > 0)
            def _():
                wait_for(z.at[ph, :, span(g), rows(r)], a2a_recv.at[ph, g])

            own = z.at[ph, :, span(g), rows(r)]
            send(own, own, ag1_send.at[ph, 0], ag1_recv.at[ph, 0, g], right)
            send(own, own, ag1_send.at[ph, 1], ag1_recv.at[ph, 1, g], left)

        def ag2(g):
            for h, q, to in ((0, q_left, right), (1, q_right, left)):
                wait_for(z.at[ph, :, span(g), rows(q)], ag1_recv.at[ph, h, g])
                passed = z.at[ph, h, span(g), rows(q)]
                send(passed, passed, ag2_send.at[ph, h], ag2_recv.at[ph, h, g], to)

        def consume(g):
            for h in range(2):
                wait_for(z.at[ph, h, span(g), rows(q_far)], ag2_recv.at[ph, h, g])

            def one(k, _):
                t = g * group + k
                slot = lax.rem(tiles - t, tiles)
                both = jnp.concatenate([spread_by[0, slot], spread_by[1, slot]], axis=1)
                (ah, al), (bh, bl) = halves(z[ph, 0, t]), halves(z[ph, 1, t])

                def square(a, b):
                    return jnp.concatenate(
                        [jnp.concatenate([a, -b], axis=1), jnp.concatenate([b, a], axis=1)], axis=0
                    )

                acc[...] += dot3(halves(both), (square(ah, bh), square(al, bl)), ((1,), (1,)))
                return 0

            lax.fori_loop(0, group, one, 0)

        def step(it, _):
            def at(lag, f):
                g = it - lag

                @pl.when((g >= 0) & (g < groups))
                def _():
                    f(g)

            at(0, produce)
            at(0, rs1)
            at(lag, ag1)
            at(1, rs2)
            at(2, settle)
            at(lag + 1, ag2)
            if ph == 0:

                @pl.when(it == lag + 2)
                def _():
                    wait_for(u, u_sem)

            at(lag + 2, consume)
            return 0

        lag = max(groups - 2, 3)
        if ph == 0:
            copy_x.wait()
            turned(x, xt)
        acc[...] = jnp.zeros_like(acc)
        if ph == 0:
            pl.semaphore_wait(barrier, tiles + 1)
        lax.fori_loop(0, groups + lag + 2, step, 0)

        for h, q_sum, q_pass in ((0, q_right, q_left), (1, q_left, q_right)):
            wait_for(part.at[h, :, rows(q_far)], rs1_send.at[ph, h])
            wait_for(part.at[:, :, rows(q_sum)], rs2_send.at[ph, h])
            wait_for(z.at[ph, :, :, rows(r)], ag1_send.at[ph, h])
            wait_for(z.at[ph, h, :, rows(q_pass)], ag2_send.at[ph, h])
        wait_for(part.at[:, pl.ds(1, tiles - 1), rows(r)], a2a_send.at[ph])

    phase(0, v, xt, lambda t: ranks[lax.rem(c + t, tiles), c], u, acc_u)
    copy_d.wait()
    for p in range(2):
        d[p] = acc_u[:, p * s : (p + 1) * s] - d[p]
    turned(d, rt)
    copy_res = pltpu.make_async_copy(d, res_any, out_sem.at[0])
    copy_res.start()
    phase(1, u, rt, lambda t: ranks[c, lax.rem(c + t, tiles)], v, acc_v)
    for p in range(2):
        grad[p] = acc_v[:, p * s : (p + 1) * s]
    copy_grad = pltpu.make_async_copy(grad, grad_any, out_sem.at[1])
    copy_grad.start()
    copy_res.wait()
    copy_grad.wait()


def plain_step(tiles, group, sources_field, data, left_basis, right_basis, ranks):
    _, n, s = sources_field.shape
    m = data.shape[1]
    k = left_basis.shape[-1]
    groups = tiles // group
    dma = pltpu.SemaphoreType.DMA
    whole = pl.BlockSpec(memory_space=pl.ANY)
    return pl.pallas_call(
        functools.partial(plain_kernel, tiles, group),
        out_shape=(
            jax.ShapeDtypeStruct((2, m, s), F32),
            jax.ShapeDtypeStruct((2, n, s), F32),
        ),
        in_specs=[pl.BlockSpec(memory_space=pltpu.SMEM)] + [whole] * 4,
        out_specs=(whole, whole),
        scratch_shapes=[
            pltpu.VMEM((2, n, s), F32),
            pltpu.VMEM((2, m, s), F32),
            pltpu.VMEM((2, tiles, m, k), F32),
            pltpu.VMEM((2, tiles, n, k), F32),
            pltpu.VMEM((2, tiles, s, k), F32),
            pltpu.VMEM((2, 2, tiles, s // 4, k), F32),
            pltpu.VMEM((2, 2, 2, tiles, s // 4, k), F32),
            pltpu.VMEM((2, 2, tiles, s, k), F32),
            pltpu.VMEM((2, 2 * s, n), BF16),
            pltpu.VMEM((2, 2 * s, m), BF16),
            pltpu.VMEM((m, 2 * s), F32),
            pltpu.VMEM((n, 2 * s), F32),
            pltpu.VMEM((2, n, s), F32),
            dma, dma, dma((groups,)), dma, dma((2,)), dma((2,)),
            dma((2, 2)), dma((2, 2)), dma((2,)), dma((2, 2)), dma((2, 2)),
            dma((2, 2, groups)), dma((2, 2, groups)), dma((2, groups)),
            dma((2, 2, groups)), dma((2, 2, groups)),
        ],
        compiler_params=pltpu.CompilerParams(
            collective_id=0, has_side_effects=True, vmem_limit_bytes=60 * 1024 * 1024
        ),
        name="tlr_plain",
    )(ranks, sources_field, data, left_basis, right_basis)


def packed_kernel(
    tiles, packs, group, ranks, x_any, d_any, u_any, v_any, res_any, grad_any,
    x, d, u, v, ucat, vcat, part, r1, r2, aout, ain00, ain01, ain10, ain11, z, xt, rt, acc_u, acc_v,
    off, tile_of, x_sem, d_sem, v_sem, u_sem, out_sem, self_sem,
    rs1_send, rs2_send, a2a_send, ag1_send, ag2_send,
    rs1_recv, rs2_recv, a2a_recv, ag1_recv, ag2_recv,
):
    c = lax.axis_index("col")
    r = lax.axis_index("row")
    thick, kmax = part.shape[-2:]
    level = kmax // 4
    s = part.shape[0] * 4 * thick
    groups = packs // group
    units = 2 * groups
    right, left = (c, lax.rem(r + 1, 4)), (c, lax.rem(r + 3, 4))
    q_right, q_left, q_far = lax.rem(r + 1, 4), lax.rem(r + 3, 4), lax.rem(r + 2, 4)
    ain = ((ain00, ain01), (ain10, ain11))

    def ahead(t):
        return lax.rem(c + t, tiles)

    def behind(t):
        return lax.rem(c + tiles - t, tiles)

    barrier = pltpu.get_barrier_semaphore()

    def greet(t, _):
        pl.semaphore_signal(barrier, inc=1, device_id=(ahead(t), r), device_id_type=MESH)
        return 0

    copy_x = pltpu.make_async_copy(x_any, x, x_sem)
    copy_x.start()

    def fetch_v(t, _):
        pltpu.make_async_copy(v_any.at[:, ahead(t)], v.at[:, t], v_sem).start()
        return 0

    lax.fori_loop(0, tiles, fetch_v, 0)
    lax.fori_loop(1, tiles, greet, 0)
    pl.semaphore_signal(barrier, inc=1, device_id=right, device_id_type=MESH)
    pl.semaphore_signal(barrier, inc=1, device_id=left, device_id_type=MESH)

    def fetch_u(t, _):
        pltpu.make_async_copy(u_any.at[:, behind(t)], u.at[:, t], u_sem).start()
        return 0

    lax.fori_loop(0, tiles, fetch_u, 0)
    copy_d = pltpu.make_async_copy(d_any, d, d_sem)
    copy_d.start()

    def tabulate(k, rank_of):
        off[k, 0] = 0

        def add(t, _):
            off[k, t + 1] = off[k, t] + rank_of(t) // level
            return 0

        lax.fori_loop(0, tiles, add, 0)

        def place(b, t):
            t = jnp.minimum(t + (b >= off[k, t + 1]).astype(jnp.int32), tiles - 1)
            tile_of[k, b] = t
            return t

        lax.fori_loop(0, 4 * packs, place, 0)

    def lanes(rows):
        return lax.broadcasted_iota(jnp.int32, (rows, kmax), 1)

    def packed(k, p, load):
        out = None
        for m in range(4):
            t = tile_of[k, 4 * p + m]
            run = pltpu.roll(load(t), (off[k, t] & 3) * level, 1)
            out = run if m == 0 else jnp.where(lanes(run.shape[0]) >= m * level, run, out)
        return out

    def pack_basis(k, basis, cat, p):
        for h in range(2):
            hi, lo = halves(packed(k, p, lambda t: basis[h, t]))
            cat[0, p, :, h * kmax : (h + 1) * kmax] = hi
            cat[1, p, :, h * kmax : (h + 1) * kmax] = lo

    def span(g):
        return pl.ds(g * group, group)

    def turned(values, dst):
        for p in range(2):
            hi, lo = halves(values[p].T)
            dst[0, p * s : (p + 1) * s] = hi
            dst[1, p * s : (p + 1) * s] = lo

    def wait_for(ref, sem):
        pltpu.make_async_copy(ref, ref, sem).wait()

    def send(src, dst, send_sem, recv_sem, to):
        pltpu.make_async_remote_copy(
            src_ref=src, dst_ref=dst, send_sem=send_sem, recv_sem=recv_sem,
            device_id=to, device_id_type=MESH,
        ).start()

    def phase(ph, makes, lhs, made_k, owner_of, spreads, spread_k, acc):
        def halved(e):
            return lax.div(e, groups), lax.rem(e, groups)

        def each(g, f):
            def one(j, _):
                f(g * group + j)
                return 0

            lax.fori_loop(0, group, one, 0)

        def produce(g):
            def one(p):
                if ph == 0:
                    pack_basis(0, v, vcat, p)
                y = dot3((lhs[0], lhs[1]), (makes[0, p], makes[1, p]), ((1,), (0,)))
                part[:, 0, :, p] = (y[:s, :kmax] + y[s:, kmax:]).reshape(2, 4, thick, kmax)
                part[:, 1, :, p] = (y[s:, :kmax] - y[:s, kmax:]).reshape(2, 4, thick, kmax)

            each(g, one)

        def rs1(e):
            f, g = halved(e)
            send(part.at[f, 0, q_far, span(g)], r1.at[ph, f, 0, span(g)],
                 rs1_send.at[ph, 0], rs1_recv.at[ph, 0, e], right)
            send(part.at[f, 1, q_far, span(g)], r1.at[ph, f, 1, span(g)],
                 rs1_send.at[ph, 1], rs1_recv.at[ph, 1, e], left)

        def rs2(e):
            f, g = halved(e)
            for h, q, to in ((0, q_right, right), (1, q_left, left)):
                wait_for(r1.at[ph, f, h, span(g)], rs1_recv.at[ph, h, e])
                part[f, h, q, span(g)] = part[f, h, q, span(g)] + r1[ph, f, h, span(g)]
                send(part.at[f, :, q, span(g)], r2.at[ph, f, h, :, span(g)],
                     rs2_send.at[ph, h], rs2_recv.at[ph, h, e], to)

        def settle(e):
            f, g = halved(e)
            for h in range(2):
                wait_for(r2.at[ph, f, h, :, span(g)], rs2_recv.at[ph, h, e])
            for h in range(2):
                part[f, h, r, span(g)] = part[f, h, r, span(g)] + (
                    r2[ph, f, 0, h, span(g)] + r2[ph, f, 1, h, span(g)]
                )

        def deal(f):
            def unpack(t, _):
                start = off[made_k, t]
                p, m = start >> 2, start & 3
                after = jnp.minimum(p + 1, packs - 1)
                for h in range(2):
                    both = jnp.where(
                        lanes(thick) >= m * level, part[f, h, r, p], part[f, h, r, after]
                    )
                    aout[f, t, h] = pltpu.roll(both, ((4 - m) & 3) * level, 1)
                return 0

            lax.fori_loop(0, tiles, unpack, 0)
            pltpu.make_async_copy(aout.at[f, 0], ain[ph][f].at[0], self_sem.at[ph, f]).start()

            def one(t, _):
                send(aout.at[f, t], ain[ph][f].at[t], a2a_send.at[ph],
                     a2a_recv.at[ph, f], (owner_of(t), r))
                return 0

            lax.fori_loop(1, tiles, one, 0)

        def gather(f):
            got = ain[ph][f]
            wait_for(got.at[0], self_sem.at[ph, f])
            wait_for(got.at[pl.ds(1, tiles - 1)], a2a_recv.at[ph, f])
            total = off[spread_k, tiles] * level

            def one(p, _):
                kept = lanes(thick) + p * kmax < total
                for h in range(2):
                    block = packed(spread_k, p, lambda t: got[t, h])
                    z[ph, f, h, r, p] = jnp.where(kept, block, 0.0)
                return 0

            lax.fori_loop(0, packs, one, 0)

        def ag1(e):
            f, g = halved(e)
            own = z.at[ph, f, :, r, span(g)]
            send(own, own, ag1_send.at[ph, 0], ag1_recv.at[ph, 0, e], right)
            send(own, own, ag1_send.at[ph, 1], ag1_recv.at[ph, 1, e], left)

        def ag2(e):
            f, g = halved(e)
            for h, q, to in ((0, q_left, right), (1, q_right, left)):
                wait_for(z.at[ph, f, :, q, span(g)], ag1_recv.at[ph, h, e])
                passed = z.at[ph, f, h, q, span(g)]
                send(passed, passed, ag2_send.at[ph, h], ag2_recv.at[ph, h, e], to)

        def consume(g):
            for f in range(2):
                for h in range(2):
                    wait_for(z.at[ph, f, h, q_far, span(g)], ag2_recv.at[ph, h, f * groups + g])

            def one(p):
                (ah, al), (bh, bl) = (
                    halves(z[ph, :, h, :, p].reshape(s, kmax)) for h in range(2)
                )

                def square(a, b):
                    return jnp.concatenate(
                        [jnp.concatenate([a, -b], axis=1), jnp.concatenate([b, a], axis=1)], axis=0
                    )

                acc[...] += dot3(
                    (spreads[0, p], spreads[1, p]), (square(ah, bh), square(al, bl)), ((1,), (1,))
                )

            each(g, one)

        lag = groups + 4

        def step(it, _):
            def at(first, count, f):
                @pl.when((it >= first) & (it < first + count))
                def _():
                    f(it - first)

            at(0, groups, produce)
            at(0, units, rs1)
            at(lag, 1, lambda _: gather(0))
            at(lag + groups, 1, lambda _: gather(1))
            at(lag, units, ag1)
            if ph == 0:

                @pl.when(it == groups)
                def _():
                    tabulate(1, lambda t: ranks[c, behind(t)])
                    wait_for(u, u_sem)

                at(groups, groups, lambda g: each(g, functools.partial(pack_basis, 1, u, ucat)))
            at(1, units, rs2)
            at(2, units, settle)
            at(groups + 1, 1, lambda _: deal(0))
            at(units + 1, 1, lambda _: deal(1))
            at(lag + 1, units, ag2)
            at(lag + 2 + groups, groups, consume)
            return 0

        acc[...] = jnp.zeros_like(acc)
        if ph == 0:
            tabulate(0, lambda t: ranks[ahead(t), c])
            copy_x.wait()
            turned(x, xt)
            wait_for(v, v_sem)
            pl.semaphore_wait(barrier, tiles + 1)
        lax.fori_loop(0, lag + units + 2, step, 0)

        for h, q_sum, q_pass in ((0, q_right, q_left), (1, q_left, q_right)):
            wait_for(part.at[:, h, q_far], rs1_send.at[ph, h])
            wait_for(part.at[:, :, q_sum], rs2_send.at[ph, h])
            wait_for(z.at[ph, :, :, r], ag1_send.at[ph, h])
            wait_for(z.at[ph, :, h, q_pass], ag2_send.at[ph, h])
        wait_for(aout.at[:, pl.ds(1, tiles - 1)], a2a_send.at[ph])

    phase(0, vcat, xt, 0, ahead, ucat, 1, acc_u)
    copy_d.wait()
    for p in range(2):
        d[p] = acc_u[:, p * s : (p + 1) * s] - d[p]
    turned(d, rt)
    copy_res = pltpu.make_async_copy(d, res_any, out_sem.at[0])
    copy_res.start()
    phase(1, ucat, rt, 1, behind, vcat, 0, acc_v)
    for p in range(2):
        x[p] = acc_v[:, p * s : (p + 1) * s]
    copy_grad = pltpu.make_async_copy(x, grad_any, out_sem.at[1])
    copy_grad.start()
    copy_res.wait()
    copy_grad.wait()


def packed_step(tiles, packs, group, collective_id, sources_field, data, left_basis, right_basis, ranks):
    _, n, s = sources_field.shape
    m = data.shape[1]
    k = left_basis.shape[-1]
    units = 2 * packs // group
    thick = s // 8
    dma = pltpu.SemaphoreType.DMA
    whole = pl.BlockSpec(memory_space=pl.ANY)
    dealt = pltpu.VMEM((tiles, 2, thick, k), F32)
    return pl.pallas_call(
        functools.partial(packed_kernel, tiles, packs, group),
        out_shape=(
            jax.ShapeDtypeStruct((2, m, s), F32),
            jax.ShapeDtypeStruct((2, n, s), F32),
        ),
        in_specs=[pl.BlockSpec(memory_space=pltpu.SMEM)] + [whole] * 4,
        out_specs=(whole, whole),
        scratch_shapes=[
            pltpu.VMEM((2, n, s), F32),
            pltpu.VMEM((2, m, s), F32),
            pltpu.VMEM((2, tiles, m, k), F32),
            pltpu.VMEM((2, tiles, n, k), F32),
            pltpu.VMEM((2, packs, m, 2 * k), BF16),
            pltpu.VMEM((2, packs, n, 2 * k), BF16),
            pltpu.VMEM((2, 2, 4, packs, thick, k), F32),
            pltpu.VMEM((2, 2, 2, packs, thick, k), F32),
            pltpu.VMEM((2, 2, 2, 2, packs, thick, k), F32),
            pltpu.VMEM((2, tiles, 2, thick, k), F32),
            dealt, dealt, dealt, dealt,
            pltpu.VMEM((2, 2, 2, 4, packs, thick, k), F32),
            pltpu.VMEM((2, 2 * s, n), BF16),
            pltpu.VMEM((2, 2 * s, m), BF16),
            pltpu.VMEM((m, 2 * s), F32),
            pltpu.VMEM((n, 2 * s), F32),
            pltpu.SMEM((2, tiles + 1), jnp.int32),
            pltpu.SMEM((2, 4 * packs), jnp.int32),
            dma, dma, dma, dma, dma((2,)), dma((2, 2)),
            dma((2, 2)), dma((2, 2)), dma((2,)), dma((2, 2)), dma((2, 2)),
            dma((2, 2, units)), dma((2, 2, units)), dma((2, 2)),
            dma((2, 2, units)), dma((2, 2, units)),
        ],
        compiler_params=pltpu.CompilerParams(
            collective_id=collective_id, has_side_effects=True, vmem_limit_bytes=60 * 1024 * 1024
        ),
        name="tlr_packed",
    )(ranks, sources_field, data, left_basis, right_basis)


def on_device(tiles, group, packs, pack_group, *args):
    runs = args[4] // (args[2].shape[-1] // 4)
    fits = jnp.maximum(runs.sum(0).max(), runs.sum(1).max()) <= 4 * packs
    return lax.cond(
        fits,
        functools.partial(packed_step, tiles, packs, pack_group, 1),
        functools.partial(plain_step, tiles, group),
        *args,
    )


def solution(mesh):
    tiles = mesh.shape["col"]
    wide = tiles % GROUP == 0 and tiles > 2 * GROUP
    packs, pack_group = (PACKS, PACK_GROUP) if wide else (tiles, 1)
    placed = P(None, ("col", "row"), None)
    bases = P(None, None, ("col", "row"), None)
    return jax.shard_map(
        functools.partial(on_device, tiles, GROUP if wide else 1, packs, pack_group),
        mesh=mesh,
        in_specs=(placed, placed, bases, bases, P()),
        out_specs=(placed, placed),
        check_vma=False,
    )
```

```python
import functools

import jax
import jax.numpy as jnp
from jax import lax
from jax.experimental import pallas as pl
from jax.experimental.pallas import tpu as pltpu
from jax.sharding import PartitionSpec as P

MESH = pl.DeviceIdType.MESH
F32 = jnp.float32
BF16 = jnp.bfloat16
GROUP = 4
PACKS = 25
PACK_GROUP = 5
UNROLL = 4
STRIDE = 11


def halves(a):
    hi = a.astype(BF16)
    return hi, (a - hi.astype(F32)).astype(BF16)


def dot3(a, b, contract):
    def dot(x, y):
        return lax.dot_general(x, y, (contract, ((), ())), preferred_element_type=F32)

    (ah, al), (bh, bl) = a, b
    return dot(ah, bh) + (dot(ah, bl) + dot(al, bh))


def plain_kernel(
    tiles, group, ranks, x_any, d_any, u_any, v_any, res_any, grad_any,
    x, d, u, v, part, r1, r2, z, xt, rt, acc_u, acc_v, grad,
    x_sem, d_sem, v_sem, u_sem, out_sem, self_sem,
    rs1_send, rs2_send, a2a_send, ag1_send, ag2_send,
    rs1_recv, rs2_recv, a2a_recv, ag1_recv, ag2_recv,
):
    c = lax.axis_index("col")
    r = lax.axis_index("row")
    s = part.shape[-2]
    quarter = s // 4
    groups = tiles // group
    right, left = (c, lax.rem(r + 1, 4)), (c, lax.rem(r + 3, 4))

    barrier = pltpu.get_barrier_semaphore()

    def greet(t, _):
        peer = (lax.rem(c + t, tiles), r)
        pl.semaphore_signal(barrier, inc=1, device_id=peer, device_id_type=MESH)
        return 0

    lax.fori_loop(1, tiles, greet, 0)
    pl.semaphore_signal(barrier, inc=1, device_id=right, device_id_type=MESH)
    pl.semaphore_signal(barrier, inc=1, device_id=left, device_id_type=MESH)

    copy_x = pltpu.make_async_copy(x_any, x, x_sem)
    copy_x.start()

    def fetch_v(t, _):
        pltpu.make_async_copy(
            v_any.at[:, lax.rem(c + t, tiles)], v.at[:, t], v_sem.at[t // group]
        ).start()
        return 0

    lax.fori_loop(0, tiles, fetch_v, 0)

    def fetch_u(t, _):
        pltpu.make_async_copy(u_any.at[:, lax.rem(c + t, tiles)], u.at[:, t], u_sem).start()
        return 0

    lax.fori_loop(0, tiles, fetch_u, 0)
    copy_d = pltpu.make_async_copy(d_any, d, d_sem)
    copy_d.start()

    def rows(q):
        return pl.ds(pl.multiple_of(q * quarter, quarter), quarter)

    def span(g):
        return pl.ds(g * group, group)

    def turned(values, dst):
        for p in range(2):
            hi, lo = halves(values[p].T)
            dst[0, p * s : (p + 1) * s] = hi
            dst[1, p * s : (p + 1) * s] = lo

    def wait_for(ref, sem):
        pltpu.make_async_copy(ref, ref, sem).wait()

    def phase(ph, made_from, lhs, rank_of, spread_by, acc):
        q_right, q_left, q_far = lax.rem(r + 1, 4), lax.rem(r + 3, 4), lax.rem(r + 2, 4)

        def send(src, dst, send_sem, recv_sem, to):
            pltpu.make_async_remote_copy(
                src_ref=src, dst_ref=dst, send_sem=send_sem, recv_sem=recv_sem,
                device_id=to, device_id_type=MESH,
            ).start()

        def produce(g):
            if ph == 0:
                wait_for(v.at[:, span(g)], v_sem.at[g])

            def one(k, _):
                t = g * group + k
                both = jnp.concatenate([made_from[0, t], made_from[1, t]], axis=1)
                y = dot3((lhs[0], lhs[1]), halves(both), ((1,), (0,)))
                kmax = y.shape[1] // 2
                level = lax.broadcasted_iota(jnp.int32, (s, kmax), 1)
                keep = level < rank_of(t)
                part[0, t] = jnp.where(keep, y[:s, :kmax] + y[s:, kmax:], 0.0)
                part[1, t] = jnp.where(keep, y[s:, :kmax] - y[:s, kmax:], 0.0)
                return 0

            lax.fori_loop(0, group, one, 0)

        def rs1(g):
            send(part.at[0, span(g), rows(q_far)], r1.at[ph, 0, span(g)],
                 rs1_send.at[ph, 0], rs1_recv.at[ph, 0, g], right)
            send(part.at[1, span(g), rows(q_far)], r1.at[ph, 1, span(g)],
                 rs1_send.at[ph, 1], rs1_recv.at[ph, 1, g], left)

        def rs2(g):
            for h, q, to in ((0, q_right, right), (1, q_left, left)):
                wait_for(r1.at[ph, h, span(g)], rs1_recv.at[ph, h, g])
                part[h, span(g), rows(q)] = part[h, span(g), rows(q)] + r1[ph, h, span(g)]
                send(part.at[:, span(g), rows(q)], r2.at[ph, h, :, span(g)],
                     rs2_send.at[ph, h], rs2_recv.at[ph, h, g], to)

        def settle(g):
            for h in range(2):
                wait_for(r2.at[ph, h, :, span(g)], rs2_recv.at[ph, h, g])
            for h in range(2):
                part[h, span(g), rows(r)] = part[h, span(g), rows(r)] + (
                    r2[ph, 0, h, span(g)] + r2[ph, 1, h, span(g)]
                )

            def one(k, _):
                t = g * group + k
                src, dst = part.at[:, t, rows(r)], z.at[ph, :, t, rows(r)]

                @pl.when(t == 0)
                def _():
                    pltpu.make_async_copy(src, dst, self_sem.at[ph]).start()

                @pl.when(t > 0)
                def _():
                    send(src, dst, a2a_send.at[ph], a2a_recv.at[ph, g], (lax.rem(c + t, tiles), r))

                return 0

            lax.fori_loop(0, group, one, 0)

        def ag1(g):
            @pl.when(g == 0)
            def _():
                wait_for(z.at[ph, :, 0, rows(r)], self_sem.at[ph])
                if group > 1:
                    wait_for(z.at[ph, :, pl.ds(1, group - 1), rows(r)], a2a_recv.at[ph, 0])

            @pl.when(g > 0)
            def _():
                wait_for(z.at[ph, :, span(g), rows(r)], a2a_recv.at[ph, g])

            own = z.at[ph, :, span(g), rows(r)]
            send(own, own, ag1_send.at[ph, 0], ag1_recv.at[ph, 0, g], right)
            send(own, own, ag1_send.at[ph, 1], ag1_recv.at[ph, 1, g], left)

        def ag2(g):
            for h, q, to in ((0, q_left, right), (1, q_right, left)):
                wait_for(z.at[ph, :, span(g), rows(q)], ag1_recv.at[ph, h, g])
                passed = z.at[ph, h, span(g), rows(q)]
                send(passed, passed, ag2_send.at[ph, h], ag2_recv.at[ph, h, g], to)

        def consume(g):
            for h in range(2):
                wait_for(z.at[ph, h, span(g), rows(q_far)], ag2_recv.at[ph, h, g])

            def one(k, _):
                t = g * group + k
                slot = lax.rem(tiles - t, tiles)
                both = jnp.concatenate([spread_by[0, slot], spread_by[1, slot]], axis=1)
                (ah, al), (bh, bl) = halves(z[ph, 0, t]), halves(z[ph, 1, t])

                def square(a, b):
                    return jnp.concatenate(
                        [jnp.concatenate([a, -b], axis=1), jnp.concatenate([b, a], axis=1)], axis=0
                    )

                acc[...] += dot3(halves(both), (square(ah, bh), square(al, bl)), ((1,), (1,)))
                return 0

            lax.fori_loop(0, group, one, 0)

        def step(it, _):
            def at(lag, f):
                g = it - lag

                @pl.when((g >= 0) & (g < groups))
                def _():
                    f(g)

            at(0, produce)
            at(0, rs1)
            at(lag, ag1)
            at(1, rs2)
            at(2, settle)
            at(lag + 1, ag2)
            if ph == 0:

                @pl.when(it == lag + 2)
                def _():
                    wait_for(u, u_sem)

            at(lag + 2, consume)
            return 0

        lag = max(groups - 2, 3)
        if ph == 0:
            copy_x.wait()
            turned(x, xt)
        acc[...] = jnp.zeros_like(acc)
        if ph == 0:
            pl.semaphore_wait(barrier, tiles + 1)
        lax.fori_loop(0, groups + lag + 2, step, 0)

        for h, q_sum, q_pass in ((0, q_right, q_left), (1, q_left, q_right)):
            wait_for(part.at[h, :, rows(q_far)], rs1_send.at[ph, h])
            wait_for(part.at[:, :, rows(q_sum)], rs2_send.at[ph, h])
            wait_for(z.at[ph, :, :, rows(r)], ag1_send.at[ph, h])
            wait_for(z.at[ph, h, :, rows(q_pass)], ag2_send.at[ph, h])
        wait_for(part.at[:, pl.ds(1, tiles - 1), rows(r)], a2a_send.at[ph])

    phase(0, v, xt, lambda t: ranks[lax.rem(c + t, tiles), c], u, acc_u)
    copy_d.wait()
    for p in range(2):
        d[p] = acc_u[:, p * s : (p + 1) * s] - d[p]
    turned(d, rt)
    copy_res = pltpu.make_async_copy(d, res_any, out_sem.at[0])
    copy_res.start()
    phase(1, u, rt, lambda t: ranks[c, lax.rem(c + t, tiles)], v, acc_v)
    for p in range(2):
        grad[p] = acc_v[:, p * s : (p + 1) * s]
    copy_grad = pltpu.make_async_copy(grad, grad_any, out_sem.at[1])
    copy_grad.start()
    copy_res.wait()
    copy_grad.wait()


def plain_step(tiles, group, sources_field, data, left_basis, right_basis, ranks):
    _, n, s = sources_field.shape
    m = data.shape[1]
    k = left_basis.shape[-1]
    groups = tiles // group
    dma = pltpu.SemaphoreType.DMA
    whole = pl.BlockSpec(memory_space=pl.ANY)
    return pl.pallas_call(
        functools.partial(plain_kernel, tiles, group),
        out_shape=(
            jax.ShapeDtypeStruct((2, m, s), F32),
            jax.ShapeDtypeStruct((2, n, s), F32),
        ),
        in_specs=[pl.BlockSpec(memory_space=pltpu.SMEM)] + [whole] * 4,
        out_specs=(whole, whole),
        scratch_shapes=[
            pltpu.VMEM((2, n, s), F32),
            pltpu.VMEM((2, m, s), F32),
            pltpu.VMEM((2, tiles, m, k), F32),
            pltpu.VMEM((2, tiles, n, k), F32),
            pltpu.VMEM((2, tiles, s, k), F32),
            pltpu.VMEM((2, 2, tiles, s // 4, k), F32),
            pltpu.VMEM((2, 2, 2, tiles, s // 4, k), F32),
            pltpu.VMEM((2, 2, tiles, s, k), F32),
            pltpu.VMEM((2, 2 * s, n), BF16),
            pltpu.VMEM((2, 2 * s, m), BF16),
            pltpu.VMEM((m, 2 * s), F32),
            pltpu.VMEM((n, 2 * s), F32),
            pltpu.VMEM((2, n, s), F32),
            dma, dma, dma((groups,)), dma, dma((2,)), dma((2,)),
            dma((2, 2)), dma((2, 2)), dma((2,)), dma((2, 2)), dma((2, 2)),
            dma((2, 2, groups)), dma((2, 2, groups)), dma((2, groups)),
            dma((2, 2, groups)), dma((2, 2, groups)),
        ],
        compiler_params=pltpu.CompilerParams(
            collective_id=0, has_side_effects=True, vmem_limit_bytes=60 * 1024 * 1024
        ),
        name="tlr_plain",
    )(ranks, sources_field, data, left_basis, right_basis)


def packed_kernel(
    tiles, packs, group, ranks, x_any, d_any, u_any, v_any, res_any, grad_any,
    x, d, u, v, ucat, vcat, part, r1, r2, aout, ain00, ain01, ain10, ain11, z, xt, rt, acc_u, acc_v,
    off, tile_of, x_sem, d_sem, v_sem, u_sem, out_sem, self_sem,
    rs1_send, rs2_send, a2a_send, ag1_send, ag2_send,
    rs1_recv, rs2_recv, a2a_recv, ag1_recv, ag2_recv,
):
    c = lax.axis_index("col")
    r = lax.axis_index("row")
    thick, kmax = part.shape[-2:]
    level = kmax // 4
    s = part.shape[0] * 4 * thick
    groups = packs // group
    units = 2 * groups
    right, left = (c, lax.rem(r + 1, 4)), (c, lax.rem(r + 3, 4))
    q_right, q_left, q_far = lax.rem(r + 1, 4), lax.rem(r + 3, 4), lax.rem(r + 2, 4)
    ain = ((ain00, ain01), (ain10, ain11))

    def ahead(t):
        return lax.rem(c + t, tiles)

    def behind(t):
        return lax.rem(c + tiles - t, tiles)

    barrier = pltpu.get_barrier_semaphore()

    def greet(t, _):
        pl.semaphore_signal(barrier, inc=1, device_id=(ahead(t), r), device_id_type=MESH)
        return 0

    copy_x = pltpu.make_async_copy(x_any, x, x_sem)
    copy_x.start()

    def fetch_v(t, _):
        pltpu.make_async_copy(v_any.at[:, ahead(t)], v.at[:, t], v_sem.at[t]).start()
        return 0

    lax.fori_loop(0, tiles, fetch_v, 0)
    lax.fori_loop(1, tiles, greet, 0)
    pl.semaphore_signal(barrier, inc=1, device_id=right, device_id_type=MESH)
    pl.semaphore_signal(barrier, inc=1, device_id=left, device_id_type=MESH)

    def fetch_u(t, _):
        pltpu.make_async_copy(u_any.at[:, behind(t)], u.at[:, t], u_sem).start()
        return 0

    copy_d = pltpu.make_async_copy(d_any, d, d_sem)

    def tabulate(k, rank_of):
        off[k, 0] = 0

        def add(t, _):
            off[k, t + 1] = off[k, t] + rank_of(t) // level
            return 0

        lax.fori_loop(0, tiles, add, 0)

        def place(b, t):
            t = jnp.minimum(t + (b >= off[k, t + 1]).astype(jnp.int32), tiles - 1)
            tile_of[k, b] = t
            return t

        lax.fori_loop(0, 4 * packs, place, 0)

    def lanes(rows):
        return lax.broadcasted_iota(jnp.int32, (rows, kmax), 1)

    def in_place(k, t, run):
        return pltpu.roll(run, (off[k, t] & 3) * level, 1)

    def packed(k, p, load):
        out = None
        for m in range(4):
            run = load(tile_of[k, 4 * p + m])
            out = run if m == 0 else jnp.where(lanes(run.shape[0]) >= m * level, run, out)
        return out

    def shift_basis(k, basis, t):
        for h in range(2):
            basis[h, t] = in_place(k, t, basis[h, t])

    def pack_basis(k, basis, cat, p):
        for h in range(2):
            hi, lo = halves(packed(k, p, lambda t: basis[h, t]))
            cat[0, p, :, h * kmax : (h + 1) * kmax] = hi
            cat[1, p, :, h * kmax : (h + 1) * kmax] = lo

    def span(g):
        return pl.ds(g * group, group)

    def turned(values, dst):
        for p in range(2):
            hi, lo = halves(values[p].T)
            dst[0, p * s : (p + 1) * s] = hi
            dst[1, p * s : (p + 1) * s] = lo

    def wait_for(ref, sem):
        pltpu.make_async_copy(ref, ref, sem).wait()

    def send(src, dst, send_sem, recv_sem, to):
        pltpu.make_async_remote_copy(
            src_ref=src, dst_ref=dst, send_sem=send_sem, recv_sem=recv_sem,
            device_id=to, device_id_type=MESH,
        ).start()

    def phase(ph, makes, lhs, made_k, owner_of, spreads, spread_k, acc):
        def halved(e):
            return lax.div(e, groups), lax.rem(e, groups)

        def each(g, f):
            def one(j, _):
                f(g * group + j)
                return 0

            lax.fori_loop(0, group, one, 0, unroll=group)

        def produce(g):
            def one(p):
                if ph == 0:
                    pack_basis(0, v, vcat, p)
                y = dot3((lhs[0], lhs[1]), (makes[0, p], makes[1, p]), ((1,), (0,)))
                part[:, 0, :, p] = (y[:s, :kmax] + y[s:, kmax:]).reshape(2, 4, thick, kmax)
                part[:, 1, :, p] = (y[s:, :kmax] - y[:s, kmax:]).reshape(2, 4, thick, kmax)

            each(g, one)

        def rs1(e):
            f, g = halved(e)
            send(part.at[f, 0, q_far, span(g)], r1.at[ph, f, 0, span(g)],
                 rs1_send.at[ph, 0], rs1_recv.at[ph, 0, e], right)
            send(part.at[f, 1, q_far, span(g)], r1.at[ph, f, 1, span(g)],
                 rs1_send.at[ph, 1], rs1_recv.at[ph, 1, e], left)

        def rs2(e):
            f, g = halved(e)
            for h, q, to in ((0, q_right, right), (1, q_left, left)):
                wait_for(r1.at[ph, f, h, span(g)], rs1_recv.at[ph, h, e])
                part[f, h, q, span(g)] = part[f, h, q, span(g)] + r1[ph, f, h, span(g)]
                send(part.at[f, :, q, span(g)], r2.at[ph, f, h, :, span(g)],
                     rs2_send.at[ph, h], rs2_recv.at[ph, h, e], to)

        def settle(e):
            f, g = halved(e)
            for h in range(2):
                wait_for(r2.at[ph, f, h, :, span(g)], rs2_recv.at[ph, h, e])
            for h in range(2):
                part[f, h, r, span(g)] = part[f, h, r, span(g)] + (
                    r2[ph, f, 0, h, span(g)] + r2[ph, f, 1, h, span(g)]
                )

        def deal(f):
            def unpack(t, _):
                start = off[made_k, t]
                p, m = start >> 2, start & 3
                after = jnp.minimum(p + 1, packs - 1)
                for h in range(2):
                    both = jnp.where(
                        lanes(thick) >= m * level, part[f, h, r, p], part[f, h, r, after]
                    )
                    aout[f, t, h] = pltpu.roll(both, ((4 - m) & 3) * level, 1)
                return 0

            lax.fori_loop(0, tiles, unpack, 0, unroll=UNROLL)
            pltpu.make_async_copy(aout.at[f, 0], ain[ph][f].at[0], self_sem.at[ph, f]).start()

            def one(j, _):
                t = lax.rem(j * STRIDE, tiles)
                send(aout.at[f, t], ain[ph][f].at[t], a2a_send.at[ph],
                     a2a_recv.at[ph, f], (owner_of(t), r))
                return 0

            lax.fori_loop(1, tiles, one, 0)

        def gather(f):
            got = ain[ph][f]
            wait_for(got.at[0], self_sem.at[ph, f])
            wait_for(got.at[pl.ds(1, tiles - 1)], a2a_recv.at[ph, f])
            total = off[spread_k, tiles] * level

            def one(p, _):
                kept = lanes(thick) + p * kmax < total
                for h in range(2):
                    block = packed(spread_k, p, lambda t: in_place(spread_k, t, got[t, h]))
                    z[ph, f, h, r, p] = jnp.where(kept, block, 0.0)
                return 0

            lax.fori_loop(0, packs, one, 0, unroll=group)

        def ag1(e):
            f, g = halved(e)
            own = z.at[ph, f, :, r, span(g)]
            send(own, own, ag1_send.at[ph, 0], ag1_recv.at[ph, 0, e], right)
            send(own, own, ag1_send.at[ph, 1], ag1_recv.at[ph, 1, e], left)

        def ag2(e):
            f, g = halved(e)
            for h, q, to in ((0, q_left, right), (1, q_right, left)):
                wait_for(z.at[ph, f, :, q, span(g)], ag1_recv.at[ph, h, e])
                passed = z.at[ph, f, h, q, span(g)]
                send(passed, passed, ag2_send.at[ph, h], ag2_recv.at[ph, h, e], to)

        def consume(g):
            for f in range(2):
                for h in range(2):
                    wait_for(z.at[ph, f, h, q_far, span(g)], ag2_recv.at[ph, h, f * groups + g])

            wide, tall = [], []
            for j in range(group):
                p = g * group + j
                (ah, al), (bh, bl) = (
                    halves(z[ph, :, h, :, p].reshape(s, kmax)) for h in range(2)
                )

                def square(a, b):
                    return jnp.concatenate(
                        [jnp.concatenate([a, -b], axis=1), jnp.concatenate([b, a], axis=1)], axis=0
                    )

                high, low = square(ah, bh), square(al, bl)
                wide += [spreads[0, p], spreads[0, p], spreads[1, p]]
                tall += [high, low, high]
            acc[...] += lax.dot_general(
                jnp.concatenate(wide, axis=1), jnp.concatenate(tall, axis=1),
                (((1,), (1,)), ((), ())), preferred_element_type=F32,
            )

        sum1, sum2, own = (1, groups + 2), (3, groups + 3), (groups + 7, 2 * groups + 7)
        passes, last = (own[0] + 2, own[1] + 2), own[1] + 3
        chunk = -(-tiles // 4)

        def step(it, _):
            def at(first, count, f, base=0):
                @pl.when((it >= first) & (it < first + count))
                def _():
                    f(it - first + base)

            def both(first, f):
                at(first[0], groups, f)
                at(first[1], groups, f, groups)

            at(0, groups, produce)
            at(0, units, rs1)
            at(own[0], 1, lambda _: gather(0))
            at(own[1], 1, lambda _: gather(1))
            both(own, ag1)
            both(sum1, rs2)
            both(passes, ag2)
            if ph == 0:
                at(groups, 1, lambda _: tabulate(1, lambda t: ranks[c, behind(t)]))
                at(groups, 1, lambda _: wait_for(u, u_sem))

                def shift(j):
                    def one(t, _):
                        shift_basis(1, u, t)
                        return 0

                    lax.fori_loop(j * chunk, jnp.minimum((j + 1) * chunk, tiles), one, 0)

                at(groups, 4, shift)
                at(groups + 4, groups, lambda g: each(g, functools.partial(pack_basis, 1, u, ucat)))
            both(sum2, settle)
            at(sum2[0] + groups - 1, 1, lambda _: deal(0))
            at(sum2[1] + groups - 1, 1, lambda _: deal(1))
            at(last, groups, consume)
            return 0

        acc[...] = jnp.zeros_like(acc)
        if ph == 0:
            tabulate(0, lambda t: ranks[ahead(t), c])
            copy_x.wait()
            turned(x, xt)

            def settle_v(t, _):
                wait_for(v.at[:, t], v_sem.at[t])
                shift_basis(0, v, t)
                return 0

            lax.fori_loop(0, tiles, settle_v, 0)
            lax.fori_loop(0, tiles, fetch_u, 0)
            copy_d.start()
            pl.semaphore_wait(barrier, tiles + 1)
        lax.fori_loop(0, last + groups, step, 0)

        for h, q_sum, q_pass in ((0, q_right, q_left), (1, q_left, q_right)):
            wait_for(part.at[:, h, q_far], rs1_send.at[ph, h])
            wait_for(part.at[:, :, q_sum], rs2_send.at[ph, h])
            wait_for(z.at[ph, :, :, r], ag1_send.at[ph, h])
            wait_for(z.at[ph, :, h, q_pass], ag2_send.at[ph, h])
        wait_for(aout.at[:, pl.ds(1, tiles - 1)], a2a_send.at[ph])

    phase(0, vcat, xt, 0, ahead, ucat, 1, acc_u)
    copy_d.wait()
    for p in range(2):
        d[p] = acc_u[:, p * s : (p + 1) * s] - d[p]
    turned(d, rt)
    copy_res = pltpu.make_async_copy(d, res_any, out_sem.at[0])
    copy_res.start()
    phase(1, ucat, rt, 1, behind, vcat, 0, acc_v)
    for p in range(2):
        x[p] = acc_v[:, p * s : (p + 1) * s]
    copy_grad = pltpu.make_async_copy(x, grad_any, out_sem.at[1])
    copy_grad.start()
    copy_res.wait()
    copy_grad.wait()


def packed_step(tiles, packs, group, collective_id, sources_field, data, left_basis, right_basis, ranks):
    _, n, s = sources_field.shape
    m = data.shape[1]
    k = left_basis.shape[-1]
    units = 2 * packs // group
    thick = s // 8
    dma = pltpu.SemaphoreType.DMA
    whole = pl.BlockSpec(memory_space=pl.ANY)
    dealt = pltpu.VMEM((tiles, 2, thick, k), F32)
    return pl.pallas_call(
        functools.partial(packed_kernel, tiles, packs, group),
        out_shape=(
            jax.ShapeDtypeStruct((2, m, s), F32),
            jax.ShapeDtypeStruct((2, n, s), F32),
        ),
        in_specs=[pl.BlockSpec(memory_space=pltpu.SMEM)] + [whole] * 4,
        out_specs=(whole, whole),
        scratch_shapes=[
            pltpu.VMEM((2, n, s), F32),
            pltpu.VMEM((2, m, s), F32),
            pltpu.VMEM((2, tiles, m, k), F32),
            pltpu.VMEM((2, tiles, n, k), F32),
            pltpu.VMEM((2, packs, m, 2 * k), BF16),
            pltpu.VMEM((2, packs, n, 2 * k), BF16),
            pltpu.VMEM((2, 2, 4, packs, thick, k), F32),
            pltpu.VMEM((2, 2, 2, packs, thick, k), F32),
            pltpu.VMEM((2, 2, 2, 2, packs, thick, k), F32),
            pltpu.VMEM((2, tiles, 2, thick, k), F32),
            dealt, dealt, dealt, dealt,
            pltpu.VMEM((2, 2, 2, 4, packs, thick, k), F32),
            pltpu.VMEM((2, 2 * s, n), BF16),
            pltpu.VMEM((2, 2 * s, m), BF16),
            pltpu.VMEM((m, 2 * s), F32),
            pltpu.VMEM((n, 2 * s), F32),
            pltpu.SMEM((2, tiles + 1), jnp.int32),
            pltpu.SMEM((2, 4 * packs), jnp.int32),
            dma, dma, dma((tiles,)), dma, dma((2,)), dma((2, 2)),
            dma((2, 2)), dma((2, 2)), dma((2,)), dma((2, 2)), dma((2, 2)),
            dma((2, 2, units)), dma((2, 2, units)), dma((2, 2)),
            dma((2, 2, units)), dma((2, 2, units)),
        ],
        compiler_params=pltpu.CompilerParams(
            collective_id=collective_id, has_side_effects=True, vmem_limit_bytes=60 * 1024 * 1024
        ),
        name="tlr_packed",
    )(ranks, sources_field, data, left_basis, right_basis)


def on_device(tiles, group, packs, pack_group, *args):
    runs = args[4] // (args[2].shape[-1] // 4)
    fits = jnp.maximum(runs.sum(0).max(), runs.sum(1).max()) <= 4 * packs
    return lax.cond(
        fits,
        functools.partial(packed_step, tiles, packs, pack_group, 1),
        functools.partial(plain_step, tiles, group),
        *args,
    )


def solution(mesh):
    tiles = mesh.shape["col"]
    wide = tiles % GROUP == 0 and tiles > 2 * GROUP
    packs, pack_group = (PACKS, PACK_GROUP) if wide else (tiles, 1)
    placed = P(None, ("col", "row"), None)
    bases = P(None, None, ("col", "row"), None)
    return jax.shard_map(
        functools.partial(on_device, tiles, GROUP if wide else 1, packs, pack_group),
        mesh=mesh,
        in_specs=(placed, placed, bases, bases, P()),
        out_specs=(placed, placed),
        check_vma=False,
    )
```

```python
import functools
import types

import jax
import jax.numpy as jnp
from jax import lax
from jax.experimental import pallas as pl
from jax.experimental.pallas import tpu as pltpu
from jax.sharding import PartitionSpec as P

MESH = pl.DeviceIdType.MESH
F32 = jnp.float32
BF16 = jnp.bfloat16
GROUP = 4
PACKS = 25
PACK_GROUP = 5
UNROLL = 4
STRIDE = 11


def halves(a):
    hi = a.astype(BF16)
    return hi, (a - hi.astype(F32)).astype(BF16)


def dot3(a, b, contract):
    def dot(x, y):
        return lax.dot_general(x, y, (contract, ((), ())), preferred_element_type=F32)

    (ah, al), (bh, bl) = a, b
    return dot(ah, bh) + (dot(ah, bl) + dot(al, bh))


def plain_kernel(
    tiles, group, ranks, x_any, d_any, u_any, v_any, res_any, grad_any,
    x, d, u, v, part, r1, r2, z, xt, rt, acc_u, acc_v, grad,
    x_sem, d_sem, v_sem, u_sem, out_sem, self_sem,
    rs1_send, rs2_send, a2a_send, ag1_send, ag2_send,
    rs1_recv, rs2_recv, a2a_recv, ag1_recv, ag2_recv,
):
    c = lax.axis_index("col")
    r = lax.axis_index("row")
    s = part.shape[-2]
    quarter = s // 4
    groups = tiles // group
    right, left = (c, lax.rem(r + 1, 4)), (c, lax.rem(r + 3, 4))

    barrier = pltpu.get_barrier_semaphore()

    def greet(t, _):
        peer = (lax.rem(c + t, tiles), r)
        pl.semaphore_signal(barrier, inc=1, device_id=peer, device_id_type=MESH)
        return 0

    lax.fori_loop(1, tiles, greet, 0)
    pl.semaphore_signal(barrier, inc=1, device_id=right, device_id_type=MESH)
    pl.semaphore_signal(barrier, inc=1, device_id=left, device_id_type=MESH)

    copy_x = pltpu.make_async_copy(x_any, x, x_sem)
    copy_x.start()

    def fetch_v(t, _):
        pltpu.make_async_copy(
            v_any.at[:, lax.rem(c + t, tiles)], v.at[:, t], v_sem.at[t // group]
        ).start()
        return 0

    lax.fori_loop(0, tiles, fetch_v, 0)

    def fetch_u(t, _):
        pltpu.make_async_copy(u_any.at[:, lax.rem(c + t, tiles)], u.at[:, t], u_sem).start()
        return 0

    lax.fori_loop(0, tiles, fetch_u, 0)
    copy_d = pltpu.make_async_copy(d_any, d, d_sem)
    copy_d.start()

    def rows(q):
        return pl.ds(pl.multiple_of(q * quarter, quarter), quarter)

    def span(g):
        return pl.ds(g * group, group)

    def turned(values, dst):
        for p in range(2):
            hi, lo = halves(values[p].T)
            dst[0, p * s : (p + 1) * s] = hi
            dst[1, p * s : (p + 1) * s] = lo

    def wait_for(ref, sem):
        pltpu.make_async_copy(ref, ref, sem).wait()

    def phase(ph, made_from, lhs, rank_of, spread_by, acc):
        q_right, q_left, q_far = lax.rem(r + 1, 4), lax.rem(r + 3, 4), lax.rem(r + 2, 4)

        def send(src, dst, send_sem, recv_sem, to):
            pltpu.make_async_remote_copy(
                src_ref=src, dst_ref=dst, send_sem=send_sem, recv_sem=recv_sem,
                device_id=to, device_id_type=MESH,
            ).start()

        def produce(g):
            if ph == 0:
                wait_for(v.at[:, span(g)], v_sem.at[g])

            def one(k, _):
                t = g * group + k
                both = jnp.concatenate([made_from[0, t], made_from[1, t]], axis=1)
                y = dot3((lhs[0], lhs[1]), halves(both), ((1,), (0,)))
                kmax = y.shape[1] // 2
                level = lax.broadcasted_iota(jnp.int32, (s, kmax), 1)
                keep = level < rank_of(t)
                part[0, t] = jnp.where(keep, y[:s, :kmax] + y[s:, kmax:], 0.0)
                part[1, t] = jnp.where(keep, y[s:, :kmax] - y[:s, kmax:], 0.0)
                return 0

            lax.fori_loop(0, group, one, 0)

        def rs1(g):
            send(part.at[0, span(g), rows(q_far)], r1.at[ph, 0, span(g)],
                 rs1_send.at[ph, 0], rs1_recv.at[ph, 0, g], right)
            send(part.at[1, span(g), rows(q_far)], r1.at[ph, 1, span(g)],
                 rs1_send.at[ph, 1], rs1_recv.at[ph, 1, g], left)

        def rs2(g):
            for h, q, to in ((0, q_right, right), (1, q_left, left)):
                wait_for(r1.at[ph, h, span(g)], rs1_recv.at[ph, h, g])
                part[h, span(g), rows(q)] = part[h, span(g), rows(q)] + r1[ph, h, span(g)]
                send(part.at[:, span(g), rows(q)], r2.at[ph, h, :, span(g)],
                     rs2_send.at[ph, h], rs2_recv.at[ph, h, g], to)

        def settle(g):
            for h in range(2):
                wait_for(r2.at[ph, h, :, span(g)], rs2_recv.at[ph, h, g])
            for h in range(2):
                part[h, span(g), rows(r)] = part[h, span(g), rows(r)] + (
                    r2[ph, 0, h, span(g)] + r2[ph, 1, h, span(g)]
                )

            def one(k, _):
                t = g * group + k
                src, dst = part.at[:, t, rows(r)], z.at[ph, :, t, rows(r)]

                @pl.when(t == 0)
                def _():
                    pltpu.make_async_copy(src, dst, self_sem.at[ph]).start()

                @pl.when(t > 0)
                def _():
                    send(src, dst, a2a_send.at[ph], a2a_recv.at[ph, g], (lax.rem(c + t, tiles), r))

                return 0

            lax.fori_loop(0, group, one, 0)

        def ag1(g):
            @pl.when(g == 0)
            def _():
                wait_for(z.at[ph, :, 0, rows(r)], self_sem.at[ph])
                if group > 1:
                    wait_for(z.at[ph, :, pl.ds(1, group - 1), rows(r)], a2a_recv.at[ph, 0])

            @pl.when(g > 0)
            def _():
                wait_for(z.at[ph, :, span(g), rows(r)], a2a_recv.at[ph, g])

            own = z.at[ph, :, span(g), rows(r)]
            send(own, own, ag1_send.at[ph, 0], ag1_recv.at[ph, 0, g], right)
            send(own, own, ag1_send.at[ph, 1], ag1_recv.at[ph, 1, g], left)

        def ag2(g):
            for h, q, to in ((0, q_left, right), (1, q_right, left)):
                wait_for(z.at[ph, :, span(g), rows(q)], ag1_recv.at[ph, h, g])
                passed = z.at[ph, h, span(g), rows(q)]
                send(passed, passed, ag2_send.at[ph, h], ag2_recv.at[ph, h, g], to)

        def consume(g):
            for h in range(2):
                wait_for(z.at[ph, h, span(g), rows(q_far)], ag2_recv.at[ph, h, g])

            def one(k, _):
                t = g * group + k
                slot = lax.rem(tiles - t, tiles)
                both = jnp.concatenate([spread_by[0, slot], spread_by[1, slot]], axis=1)
                (ah, al), (bh, bl) = halves(z[ph, 0, t]), halves(z[ph, 1, t])

                def square(a, b):
                    return jnp.concatenate(
                        [jnp.concatenate([a, -b], axis=1), jnp.concatenate([b, a], axis=1)], axis=0
                    )

                acc[...] += dot3(halves(both), (square(ah, bh), square(al, bl)), ((1,), (1,)))
                return 0

            lax.fori_loop(0, group, one, 0)

        def step(it, _):
            def at(lag, f):
                g = it - lag

                @pl.when((g >= 0) & (g < groups))
                def _():
                    f(g)

            at(0, produce)
            at(0, rs1)
            at(lag, ag1)
            at(1, rs2)
            at(2, settle)
            at(lag + 1, ag2)
            if ph == 0:

                @pl.when(it == lag + 2)
                def _():
                    wait_for(u, u_sem)

            at(lag + 2, consume)
            return 0

        lag = max(groups - 2, 3)
        if ph == 0:
            copy_x.wait()
            turned(x, xt)
        acc[...] = jnp.zeros_like(acc)
        if ph == 0:
            pl.semaphore_wait(barrier, tiles + 1)
        lax.fori_loop(0, groups + lag + 2, step, 0)

        for h, q_sum, q_pass in ((0, q_right, q_left), (1, q_left, q_right)):
            wait_for(part.at[h, :, rows(q_far)], rs1_send.at[ph, h])
            wait_for(part.at[:, :, rows(q_sum)], rs2_send.at[ph, h])
            wait_for(z.at[ph, :, :, rows(r)], ag1_send.at[ph, h])
            wait_for(z.at[ph, h, :, rows(q_pass)], ag2_send.at[ph, h])
        wait_for(part.at[:, pl.ds(1, tiles - 1), rows(r)], a2a_send.at[ph])

    phase(0, v, xt, lambda t: ranks[lax.rem(c + t, tiles), c], u, acc_u)
    copy_d.wait()
    for p in range(2):
        d[p] = acc_u[:, p * s : (p + 1) * s] - d[p]
    turned(d, rt)
    copy_res = pltpu.make_async_copy(d, res_any, out_sem.at[0])
    copy_res.start()
    phase(1, u, rt, lambda t: ranks[c, lax.rem(c + t, tiles)], v, acc_v)
    for p in range(2):
        grad[p] = acc_v[:, p * s : (p + 1) * s]
    copy_grad = pltpu.make_async_copy(grad, grad_any, out_sem.at[1])
    copy_grad.start()
    copy_res.wait()
    copy_grad.wait()


def plain_step(tiles, group, sources_field, data, left_basis, right_basis, ranks):
    _, n, s = sources_field.shape
    m = data.shape[1]
    k = left_basis.shape[-1]
    groups = tiles // group
    dma = pltpu.SemaphoreType.DMA
    whole = pl.BlockSpec(memory_space=pl.ANY)
    return pl.pallas_call(
        functools.partial(plain_kernel, tiles, group),
        out_shape=(
            jax.ShapeDtypeStruct((2, m, s), F32),
            jax.ShapeDtypeStruct((2, n, s), F32),
        ),
        in_specs=[pl.BlockSpec(memory_space=pltpu.SMEM)] + [whole] * 4,
        out_specs=(whole, whole),
        scratch_shapes=[
            pltpu.VMEM((2, n, s), F32),
            pltpu.VMEM((2, m, s), F32),
            pltpu.VMEM((2, tiles, m, k), F32),
            pltpu.VMEM((2, tiles, n, k), F32),
            pltpu.VMEM((2, tiles, s, k), F32),
            pltpu.VMEM((2, 2, tiles, s // 4, k), F32),
            pltpu.VMEM((2, 2, 2, tiles, s // 4, k), F32),
            pltpu.VMEM((2, 2, tiles, s, k), F32),
            pltpu.VMEM((2, 2 * s, n), BF16),
            pltpu.VMEM((2, 2 * s, m), BF16),
            pltpu.VMEM((m, 2 * s), F32),
            pltpu.VMEM((n, 2 * s), F32),
            pltpu.VMEM((2, n, s), F32),
            dma, dma, dma((groups,)), dma, dma((2,)), dma((2,)),
            dma((2, 2)), dma((2, 2)), dma((2,)), dma((2, 2)), dma((2, 2)),
            dma((2, 2, groups)), dma((2, 2, groups)), dma((2, groups)),
            dma((2, 2, groups)), dma((2, 2, groups)),
        ],
        compiler_params=pltpu.CompilerParams(
            collective_id=0, has_side_effects=True, vmem_limit_bytes=60 * 1024 * 1024
        ),
        name="tlr_plain",
    )(ranks, sources_field, data, left_basis, right_basis)


def packed_kernel(
    tiles, packs, group, ranks, x_any, d_any, u_any, v_any, res_any, grad_any,
    x, d, u, v, ucat, vcat, part, r1, r2, aout, ain00, ain01, ain10, ain11, z, xt, rt, acc_u, acc_v,
    off, tile_of, x_sem, d_sem, v_sem, u_sem, out_sem, self_sem,
    rs1_send, rs2_send, a2a_send, ag1_send, ag2_send,
    rs1_recv, rs2_recv, a2a_recv, ag1_recv, ag2_recv,
):
    c = lax.axis_index("col")
    r = lax.axis_index("row")
    thick, kmax = part.shape[-2:]
    level = kmax // 4
    s = part.shape[0] * 4 * thick
    groups = packs // group
    units = 2 * groups
    right, left = (c, lax.rem(r + 1, 4)), (c, lax.rem(r + 3, 4))
    q_right, q_left, q_far = lax.rem(r + 1, 4), lax.rem(r + 3, 4), lax.rem(r + 2, 4)
    ain = ((ain00, ain01), (ain10, ain11))

    def ahead(t):
        return lax.rem(c + t, tiles)

    def behind(t):
        return lax.rem(c + tiles - t, tiles)

    barrier = pltpu.get_barrier_semaphore()

    def greet(t, _):
        pl.semaphore_signal(barrier, inc=1, device_id=(ahead(t), r), device_id_type=MESH)
        return 0

    copy_x = pltpu.make_async_copy(x_any, x, x_sem)
    copy_x.start()

    def fetch_v(t, _):
        pltpu.make_async_copy(v_any.at[:, ahead(t)], v.at[:, t], v_sem.at[t]).start()
        return 0

    lax.fori_loop(0, tiles, fetch_v, 0)
    lax.fori_loop(1, tiles, greet, 0)
    pl.semaphore_signal(barrier, inc=1, device_id=right, device_id_type=MESH)
    pl.semaphore_signal(barrier, inc=1, device_id=left, device_id_type=MESH)

    def fetch_u(t, _):
        pltpu.make_async_copy(u_any.at[:, behind(t)], u.at[:, t], u_sem).start()
        return 0

    copy_d = pltpu.make_async_copy(d_any, d, d_sem)

    def tabulate(k, rank_of):
        off[k, 0] = 0

        def add(t, _):
            off[k, t + 1] = off[k, t] + rank_of(t) // level
            return 0

        lax.fori_loop(0, tiles, add, 0)

        def place(b, t):
            t = jnp.minimum(t + (b >= off[k, t + 1]).astype(jnp.int32), tiles - 1)
            tile_of[k, b] = t
            return t

        lax.fori_loop(0, 4 * packs, place, 0)

    def lanes(rows):
        return lax.broadcasted_iota(jnp.int32, (rows, kmax), 1)

    def in_place(k, t, run):
        return pltpu.roll(run, (off[k, t] & 3) * level, 1)

    def packed(k, p, load):
        out = None
        for m in range(4):
            run = load(tile_of[k, 4 * p + m])
            out = run if m == 0 else jnp.where(lanes(run.shape[0]) >= m * level, run, out)
        return out

    def shift_basis(k, basis, t):
        for h in range(2):
            basis[h, t] = in_place(k, t, basis[h, t])

    def pack_basis(k, basis, cat, p):
        for h in range(2):
            hi, lo = halves(packed(k, p, lambda t: basis[h, t]))
            cat[0, p, :, h * kmax : (h + 1) * kmax] = hi
            cat[1, p, :, h * kmax : (h + 1) * kmax] = lo

    def span(g):
        return pl.ds(g * group, group)

    def wait_for(ref, sem):
        pltpu.make_async_copy(ref, ref, sem).wait()

    def send(src, dst, send_sem, recv_sem, to):
        pltpu.make_async_remote_copy(
            src_ref=src, dst_ref=dst, send_sem=send_sem, recv_sem=recv_sem,
            device_id=to, device_id_type=MESH,
        ).start()

    def phase(ph, makes, made_k, owner_of, spreads, spread_k):
        def halved(e):
            return lax.div(e, groups), lax.rem(e, groups)

        def each(g, f):
            def one(j, _):
                f(g * group + j)
                return 0

            lax.fori_loop(0, group, one, 0, unroll=group)

        def produce(g):
            def one(p):
                pack_basis(0, v, vcat, p)
                y = dot3((xt[0], xt[1]), (makes[0, p], makes[1, p]), ((1,), (0,)))
                part[:, 0, :, p] = (y[:s, :kmax] + y[s:, kmax:]).reshape(2, 4, thick, kmax)
                part[:, 1, :, p] = (y[s:, :kmax] - y[:s, kmax:]).reshape(2, 4, thick, kmax)

            each(g, one)

        def produce_half(f, g):
            n = s // 2

            def one(p):
                y = dot3((rt[f, 0], rt[f, 1]), (makes[0, p], makes[1, p]), ((1,), (0,)))
                part[f, 0, :, p] = (y[:n, :kmax] + y[n:, kmax:]).reshape(4, thick, kmax)
                part[f, 1, :, p] = (y[n:, :kmax] - y[:n, kmax:]).reshape(4, thick, kmax)

            each(g, one)

        def sums_sent(f):
            for h, q in ((0, q_right), (1, q_left)):
                wait_for(part.at[f, h, q_far], rs1_send.at[ph, f, h])
                wait_for(part.at[f, :, q], rs2_send.at[ph, f, h])

        def dealt(f):
            wait_for(aout.at[f, pl.ds(1, tiles - 1)], a2a_send.at[ph, f])

        def gathered():
            for h, q in ((0, q_left), (1, q_right)):
                wait_for(z.at[ph, :, :, r], ag1_send.at[ph, h])
                wait_for(z.at[ph, :, h, q], ag2_send.at[ph, h])

        def rs1(e):
            f, g = halved(e)
            send(part.at[f, 0, q_far, span(g)], r1.at[ph, f, 0, span(g)],
                 rs1_send.at[ph, f, 0], rs1_recv.at[ph, 0, e], right)
            send(part.at[f, 1, q_far, span(g)], r1.at[ph, f, 1, span(g)],
                 rs1_send.at[ph, f, 1], rs1_recv.at[ph, 1, e], left)

        def rs2(e):
            f, g = halved(e)
            for h, q, to in ((0, q_right, right), (1, q_left, left)):
                wait_for(r1.at[ph, f, h, span(g)], rs1_recv.at[ph, h, e])
                part[f, h, q, span(g)] = part[f, h, q, span(g)] + r1[ph, f, h, span(g)]
                send(part.at[f, :, q, span(g)], r2.at[ph, f, h, :, span(g)],
                     rs2_send.at[ph, f, h], rs2_recv.at[ph, h, e], to)

        def settle(e):
            f, g = halved(e)
            for h in range(2):
                wait_for(r2.at[ph, f, h, :, span(g)], rs2_recv.at[ph, h, e])
            for h in range(2):
                part[f, h, r, span(g)] = part[f, h, r, span(g)] + (
                    r2[ph, f, 0, h, span(g)] + r2[ph, f, 1, h, span(g)]
                )

        def deal(f):
            def unpack(t, _):
                start = off[made_k, t]
                p, m = start >> 2, start & 3
                after = jnp.minimum(p + 1, packs - 1)
                for h in range(2):
                    both = jnp.where(
                        lanes(thick) >= m * level, part[f, h, r, p], part[f, h, r, after]
                    )
                    aout[f, t, h] = pltpu.roll(both, ((4 - m) & 3) * level, 1)
                return 0

            lax.fori_loop(0, tiles, unpack, 0, unroll=UNROLL)
            pltpu.make_async_copy(aout.at[f, 0], ain[ph][f].at[0], self_sem.at[ph, f]).start()

            def one(j, _):
                t = lax.rem(j * STRIDE, tiles)
                send(aout.at[f, t], ain[ph][f].at[t], a2a_send.at[ph, f],
                     a2a_recv.at[ph, f], (owner_of(t), r))
                return 0

            lax.fori_loop(1, tiles, one, 0)

        def gather(f):
            got = ain[ph][f]
            wait_for(got.at[0], self_sem.at[ph, f])
            wait_for(got.at[pl.ds(1, tiles - 1)], a2a_recv.at[ph, f])
            total = off[spread_k, tiles] * level

            def one(p, _):
                kept = lanes(thick) + p * kmax < total
                for h in range(2):
                    block = packed(spread_k, p, lambda t: in_place(spread_k, t, got[t, h]))
                    z[ph, f, h, r, p] = jnp.where(kept, block, 0.0)
                return 0

            lax.fori_loop(0, packs, one, 0, unroll=group)

        def ag1(e):
            f, g = halved(e)
            own = z.at[ph, f, :, r, span(g)]
            send(own, own, ag1_send.at[ph, 0], ag1_recv.at[ph, 0, e], right)
            send(own, own, ag1_send.at[ph, 1], ag1_recv.at[ph, 1, e], left)

        def ag2(e):
            f, g = halved(e)
            for h, q, to in ((0, q_left, right), (1, q_right, left)):
                wait_for(z.at[ph, f, :, q, span(g)], ag1_recv.at[ph, h, e])
                passed = z.at[ph, f, h, q, span(g)]
                send(passed, passed, ag2_send.at[ph, h], ag2_recv.at[ph, h, e], to)

        def arrived(f, g):
            for h in range(2):
                wait_for(z.at[ph, f, h, q_far, span(g)], ag2_recv.at[ph, h, f * groups + g])

        def spread(g, coeffs):
            wide, tall = [], []
            for j in range(group):
                p = g * group + j
                (ah, al), (bh, bl) = (halves(coeffs(h, p)) for h in range(2))

                def square(a, b):
                    return jnp.concatenate(
                        [jnp.concatenate([a, -b], axis=1), jnp.concatenate([b, a], axis=1)], axis=0
                    )

                high, low = square(ah, bh), square(al, bl)
                wide += [spreads[0, p], spreads[0, p], spreads[1, p]]
                tall += [high, low, high]
            return lax.dot_general(
                jnp.concatenate(wide, axis=1), jnp.concatenate(tall, axis=1),
                (((1,), (1,)), ((), ())), preferred_element_type=F32,
            )

        def consume(g):
            for f in range(2):
                arrived(f, g)
            acc_v[...] += spread(g, lambda h, p: z[ph, :, h, :, p].reshape(s, kmax))

        def consume_half(f, g):
            arrived(f, g)
            acc_u[f] += spread(g, lambda h, p: z[ph, f, h, :, p].reshape(s // 2, kmax))

        return types.SimpleNamespace(**locals())

    fwd = phase(0, vcat, 0, ahead, ucat, 1)
    adj = phase(1, ucat, 1, behind, vcat, 0)

    def subtract(f):
        n = s // 2
        given = jnp.concatenate([d[h, :, f * n : (f + 1) * n] for h in range(2)], axis=1)
        rest = acc_u[f] - given
        hi, lo = halves(rest.T)
        rt[f, 0] = hi
        rt[f, 1] = lo
        for h in range(2):
            d[h, :, f * n : (f + 1) * n] = rest[:, h * n : (h + 1) * n]

    sum1, sum2, own = (2, groups + 2), (4, groups + 4), (groups + 7, 2 * groups + 7)
    passes, used = (own[0] + 2, own[1] + 2), (own[0] + 4, own[1] + 4)
    second = used[0] + groups
    chunk = -(-tiles // 4)

    def step(it, _):
        def at(first, count, f, base=0):
            @pl.when((it >= first) & (it < first + count))
            def _():
                f(it - first + base)

        def both(first, f):
            at(first[0], groups, f)
            at(first[1], groups, f, groups)

        def once(when, f, *given):
            at(when, 1, lambda _: f(*given))

        def later(pair):
            return tuple(first + second for first in pair)

        at(0, groups, fwd.produce)
        at(0, units, fwd.rs1)
        once(own[0], fwd.gather, 0)
        once(own[1], fwd.gather, 1)
        both(own, fwd.ag1)
        both(sum1, fwd.rs2)
        both(passes, fwd.ag2)
        once(groups, tabulate, 1, lambda t: ranks[c, behind(t)])
        once(groups, wait_for, u, u_sem)

        def shift(j):
            def one(t, _):
                shift_basis(1, u, t)
                return 0

            lax.fori_loop(j * chunk, jnp.minimum((j + 1) * chunk, tiles), one, 0)

        at(groups, 4, shift)
        at(groups + 4, groups, lambda g: fwd.each(g, functools.partial(pack_basis, 1, u, ucat)))
        both(sum2, fwd.settle)
        for f in range(2):
            once(sum2[f] + groups - 1, fwd.deal, f)
        once(used[0], copy_d.wait)
        for f in range(2):
            at(used[f], groups, functools.partial(fwd.consume_half, f))
            once(used[f] + groups - 1, subtract, f)

        for f in range(2):
            once(second + f * groups, fwd.sums_sent, f)
            at(second + f * groups, groups, functools.partial(adj.produce_half, f))
        at(second, units, adj.rs1)
        once(second + own[0], adj.gather, 0)
        once(second + own[1], adj.gather, 1)
        both(later(own), adj.ag1)
        both(later(sum1), adj.rs2)
        both(later(passes), adj.ag2)
        both(later(sum2), adj.settle)
        for f in range(2):
            once(second + sum2[f] + groups - 1, fwd.dealt, f)
            once(second + sum2[f] + groups - 1, adj.deal, f)
        once(second + 2 * groups, lambda: copy_res.start())
        at(second + used[1], groups, adj.consume)
        return 0

    copy_res = pltpu.make_async_copy(d, res_any, out_sem.at[0])
    acc_u[...] = jnp.zeros_like(acc_u)
    acc_v[...] = jnp.zeros_like(acc_v)
    tabulate(0, lambda t: ranks[ahead(t), c])
    copy_x.wait()
    for p in range(2):
        hi, lo = halves(x[p].T)
        xt[0, p * s : (p + 1) * s] = hi
        xt[1, p * s : (p + 1) * s] = lo

    def settle_v(t, _):
        wait_for(v.at[:, t], v_sem.at[t])
        shift_basis(0, v, t)
        return 0

    lax.fori_loop(0, tiles, settle_v, 0)
    lax.fori_loop(0, tiles, fetch_u, 0)
    copy_d.start()
    pl.semaphore_wait(barrier, tiles + 1)
    lax.fori_loop(0, second + used[1] + groups, step, 0)

    for p in range(2):
        x[p] = acc_v[:, p * s : (p + 1) * s]
    copy_grad = pltpu.make_async_copy(x, grad_any, out_sem.at[1])
    copy_grad.start()
    fwd.gathered()
    adj.gathered()
    for f in range(2):
        adj.sums_sent(f)
        adj.dealt(f)
    copy_res.wait()
    copy_grad.wait()


def packed_step(tiles, packs, group, collective_id, sources_field, data, left_basis, right_basis, ranks):
    _, n, s = sources_field.shape
    m = data.shape[1]
    k = left_basis.shape[-1]
    units = 2 * packs // group
    thick = s // 8
    dma = pltpu.SemaphoreType.DMA
    whole = pl.BlockSpec(memory_space=pl.ANY)
    dealt = pltpu.VMEM((tiles, 2, thick, k), F32)
    return pl.pallas_call(
        functools.partial(packed_kernel, tiles, packs, group),
        out_shape=(
            jax.ShapeDtypeStruct((2, m, s), F32),
            jax.ShapeDtypeStruct((2, n, s), F32),
        ),
        in_specs=[pl.BlockSpec(memory_space=pltpu.SMEM)] + [whole] * 4,
        out_specs=(whole, whole),
        scratch_shapes=[
            pltpu.VMEM((2, n, s), F32),
            pltpu.VMEM((2, m, s), F32),
            pltpu.VMEM((2, tiles, m, k), F32),
            pltpu.VMEM((2, tiles, n, k), F32),
            pltpu.VMEM((2, packs, m, 2 * k), BF16),
            pltpu.VMEM((2, packs, n, 2 * k), BF16),
            pltpu.VMEM((2, 2, 4, packs, thick, k), F32),
            pltpu.VMEM((2, 2, 2, packs, thick, k), F32),
            pltpu.VMEM((2, 2, 2, 2, packs, thick, k), F32),
            pltpu.VMEM((2, tiles, 2, thick, k), F32),
            dealt, dealt, dealt, dealt,
            pltpu.VMEM((2, 2, 2, 4, packs, thick, k), F32),
            pltpu.VMEM((2, 2 * s, n), BF16),
            pltpu.VMEM((2, 2, s, m), BF16),
            pltpu.VMEM((2, m, s), F32),
            pltpu.VMEM((n, 2 * s), F32),
            pltpu.SMEM((2, tiles + 1), jnp.int32),
            pltpu.SMEM((2, 4 * packs), jnp.int32),
            dma, dma, dma((tiles,)), dma, dma((2,)), dma((2, 2)),
            dma((2, 2, 2)), dma((2, 2, 2)), dma((2, 2)), dma((2, 2)), dma((2, 2)),
            dma((2, 2, units)), dma((2, 2, units)), dma((2, 2)),
            dma((2, 2, units)), dma((2, 2, units)),
        ],
        compiler_params=pltpu.CompilerParams(
            collective_id=collective_id, has_side_effects=True, vmem_limit_bytes=60 * 1024 * 1024
        ),
        name="tlr_packed",
    )(ranks, sources_field, data, left_basis, right_basis)


def on_device(tiles, group, packs, pack_group, *args):
    runs = args[4] // (args[2].shape[-1] // 4)
    fits = jnp.maximum(runs.sum(0).max(), runs.sum(1).max()) <= 4 * packs
    return lax.cond(
        fits,
        functools.partial(packed_step, tiles, packs, pack_group, 1),
        functools.partial(plain_step, tiles, group),
        *args,
    )


def solution(mesh):
    tiles = mesh.shape["col"]
    wide = tiles % GROUP == 0 and tiles > 2 * GROUP
    packs, pack_group = (PACKS, PACK_GROUP) if wide else (tiles, 1)
    placed = P(None, ("col", "row"), None)
    bases = P(None, None, ("col", "row"), None)
    return jax.shard_map(
        functools.partial(on_device, tiles, GROUP if wide else 1, packs, pack_group),
        mesh=mesh,
        in_specs=(placed, placed, bases, bases, P()),
        out_specs=(placed, placed),
        check_vma=False,
    )
```

```python
import functools
import types

import jax
import jax.numpy as jnp
from jax import lax
from jax.experimental import pallas as pl
from jax.experimental.pallas import tpu as pltpu
from jax.sharding import PartitionSpec as P

MESH = pl.DeviceIdType.MESH
F32 = jnp.float32
BF16 = jnp.bfloat16
GROUP = 4
SIZES = ((24, 6), (25, 5))
UNROLL = 4
STRIDE = 11


def halves(a):
    hi = a.astype(BF16)
    return hi, (a - hi.astype(F32)).astype(BF16)


def dot3(a, b, contract):
    def dot(x, y):
        return lax.dot_general(x, y, (contract, ((), ())), preferred_element_type=F32)

    (ah, al), (bh, bl) = a, b
    return dot(ah, bh) + (dot(ah, bl) + dot(al, bh))


def plain_kernel(
    tiles, group, ranks, x_any, d_any, u_any, v_any, res_any, grad_any,
    x, d, u, v, part, r1, r2, z, xt, rt, acc_u, acc_v, grad,
    x_sem, d_sem, v_sem, u_sem, out_sem, self_sem,
    rs1_send, rs2_send, a2a_send, ag1_send, ag2_send,
    rs1_recv, rs2_recv, a2a_recv, ag1_recv, ag2_recv,
):
    c = lax.axis_index("col")
    r = lax.axis_index("row")
    s = part.shape[-2]
    quarter = s // 4
    groups = tiles // group
    right, left = (c, lax.rem(r + 1, 4)), (c, lax.rem(r + 3, 4))

    barrier = pltpu.get_barrier_semaphore()

    def greet(t, _):
        peer = (lax.rem(c + t, tiles), r)
        pl.semaphore_signal(barrier, inc=1, device_id=peer, device_id_type=MESH)
        return 0

    lax.fori_loop(1, tiles, greet, 0)
    pl.semaphore_signal(barrier, inc=1, device_id=right, device_id_type=MESH)
    pl.semaphore_signal(barrier, inc=1, device_id=left, device_id_type=MESH)

    copy_x = pltpu.make_async_copy(x_any, x, x_sem)
    copy_x.start()

    def fetch_v(t, _):
        pltpu.make_async_copy(
            v_any.at[:, lax.rem(c + t, tiles)], v.at[:, t], v_sem.at[t // group]
        ).start()
        return 0

    lax.fori_loop(0, tiles, fetch_v, 0)

    def fetch_u(t, _):
        pltpu.make_async_copy(u_any.at[:, lax.rem(c + t, tiles)], u.at[:, t], u_sem).start()
        return 0

    lax.fori_loop(0, tiles, fetch_u, 0)
    copy_d = pltpu.make_async_copy(d_any, d, d_sem)
    copy_d.start()

    def rows(q):
        return pl.ds(pl.multiple_of(q * quarter, quarter), quarter)

    def span(g):
        return pl.ds(g * group, group)

    def turned(values, dst):
        for p in range(2):
            hi, lo = halves(values[p].T)
            dst[0, p * s : (p + 1) * s] = hi
            dst[1, p * s : (p + 1) * s] = lo

    def wait_for(ref, sem):
        pltpu.make_async_copy(ref, ref, sem).wait()

    def phase(ph, made_from, lhs, rank_of, spread_by, acc):
        q_right, q_left, q_far = lax.rem(r + 1, 4), lax.rem(r + 3, 4), lax.rem(r + 2, 4)

        def send(src, dst, send_sem, recv_sem, to):
            pltpu.make_async_remote_copy(
                src_ref=src, dst_ref=dst, send_sem=send_sem, recv_sem=recv_sem,
                device_id=to, device_id_type=MESH,
            ).start()

        def produce(g):
            if ph == 0:
                wait_for(v.at[:, span(g)], v_sem.at[g])

            def one(k, _):
                t = g * group + k
                both = jnp.concatenate([made_from[0, t], made_from[1, t]], axis=1)
                y = dot3((lhs[0], lhs[1]), halves(both), ((1,), (0,)))
                kmax = y.shape[1] // 2
                level = lax.broadcasted_iota(jnp.int32, (s, kmax), 1)
                keep = level < rank_of(t)
                part[0, t] = jnp.where(keep, y[:s, :kmax] + y[s:, kmax:], 0.0)
                part[1, t] = jnp.where(keep, y[s:, :kmax] - y[:s, kmax:], 0.0)
                return 0

            lax.fori_loop(0, group, one, 0)

        def rs1(g):
            send(part.at[0, span(g), rows(q_far)], r1.at[ph, 0, span(g)],
                 rs1_send.at[ph, 0], rs1_recv.at[ph, 0, g], right)
            send(part.at[1, span(g), rows(q_far)], r1.at[ph, 1, span(g)],
                 rs1_send.at[ph, 1], rs1_recv.at[ph, 1, g], left)

        def rs2(g):
            for h, q, to in ((0, q_right, right), (1, q_left, left)):
                wait_for(r1.at[ph, h, span(g)], rs1_recv.at[ph, h, g])
                part[h, span(g), rows(q)] = part[h, span(g), rows(q)] + r1[ph, h, span(g)]
                send(part.at[:, span(g), rows(q)], r2.at[ph, h, :, span(g)],
                     rs2_send.at[ph, h], rs2_recv.at[ph, h, g], to)

        def settle(g):
            for h in range(2):
                wait_for(r2.at[ph, h, :, span(g)], rs2_recv.at[ph, h, g])
            for h in range(2):
                part[h, span(g), rows(r)] = part[h, span(g), rows(r)] + (
                    r2[ph, 0, h, span(g)] + r2[ph, 1, h, span(g)]
                )

            def one(k, _):
                t = g * group + k
                src, dst = part.at[:, t, rows(r)], z.at[ph, :, t, rows(r)]

                @pl.when(t == 0)
                def _():
                    pltpu.make_async_copy(src, dst, self_sem.at[ph]).start()

                @pl.when(t > 0)
                def _():
                    send(src, dst, a2a_send.at[ph], a2a_recv.at[ph, g], (lax.rem(c + t, tiles), r))

                return 0

            lax.fori_loop(0, group, one, 0)

        def ag1(g):
            @pl.when(g == 0)
            def _():
                wait_for(z.at[ph, :, 0, rows(r)], self_sem.at[ph])
                if group > 1:
                    wait_for(z.at[ph, :, pl.ds(1, group - 1), rows(r)], a2a_recv.at[ph, 0])

            @pl.when(g > 0)
            def _():
                wait_for(z.at[ph, :, span(g), rows(r)], a2a_recv.at[ph, g])

            own = z.at[ph, :, span(g), rows(r)]
            send(own, own, ag1_send.at[ph, 0], ag1_recv.at[ph, 0, g], right)
            send(own, own, ag1_send.at[ph, 1], ag1_recv.at[ph, 1, g], left)

        def ag2(g):
            for h, q, to in ((0, q_left, right), (1, q_right, left)):
                wait_for(z.at[ph, :, span(g), rows(q)], ag1_recv.at[ph, h, g])
                passed = z.at[ph, h, span(g), rows(q)]
                send(passed, passed, ag2_send.at[ph, h], ag2_recv.at[ph, h, g], to)

        def consume(g):
            for h in range(2):
                wait_for(z.at[ph, h, span(g), rows(q_far)], ag2_recv.at[ph, h, g])

            def one(k, _):
                t = g * group + k
                slot = lax.rem(tiles - t, tiles)
                both = jnp.concatenate([spread_by[0, slot], spread_by[1, slot]], axis=1)
                (ah, al), (bh, bl) = halves(z[ph, 0, t]), halves(z[ph, 1, t])

                def square(a, b):
                    return jnp.concatenate(
                        [jnp.concatenate([a, -b], axis=1), jnp.concatenate([b, a], axis=1)], axis=0
                    )

                acc[...] += dot3(halves(both), (square(ah, bh), square(al, bl)), ((1,), (1,)))
                return 0

            lax.fori_loop(0, group, one, 0)

        def step(it, _):
            def at(lag, f):
                g = it - lag

                @pl.when((g >= 0) & (g < groups))
                def _():
                    f(g)

            at(0, produce)
            at(0, rs1)
            at(lag, ag1)
            at(1, rs2)
            at(2, settle)
            at(lag + 1, ag2)
            if ph == 0:

                @pl.when(it == lag + 2)
                def _():
                    wait_for(u, u_sem)

            at(lag + 2, consume)
            return 0

        lag = max(groups - 2, 3)
        if ph == 0:
            copy_x.wait()
            turned(x, xt)
        acc[...] = jnp.zeros_like(acc)
        if ph == 0:
            pl.semaphore_wait(barrier, tiles + 1)
        lax.fori_loop(0, groups + lag + 2, step, 0)

        for h, q_sum, q_pass in ((0, q_right, q_left), (1, q_left, q_right)):
            wait_for(part.at[h, :, rows(q_far)], rs1_send.at[ph, h])
            wait_for(part.at[:, :, rows(q_sum)], rs2_send.at[ph, h])
            wait_for(z.at[ph, :, :, rows(r)], ag1_send.at[ph, h])
            wait_for(z.at[ph, h, :, rows(q_pass)], ag2_send.at[ph, h])
        wait_for(part.at[:, pl.ds(1, tiles - 1), rows(r)], a2a_send.at[ph])

    phase(0, v, xt, lambda t: ranks[lax.rem(c + t, tiles), c], u, acc_u)
    copy_d.wait()
    for p in range(2):
        d[p] = acc_u[:, p * s : (p + 1) * s] - d[p]
    turned(d, rt)
    copy_res = pltpu.make_async_copy(d, res_any, out_sem.at[0])
    copy_res.start()
    phase(1, u, rt, lambda t: ranks[c, lax.rem(c + t, tiles)], v, acc_v)
    for p in range(2):
        grad[p] = acc_v[:, p * s : (p + 1) * s]
    copy_grad = pltpu.make_async_copy(grad, grad_any, out_sem.at[1])
    copy_grad.start()
    copy_res.wait()
    copy_grad.wait()


def plain_step(tiles, group, sources_field, data, left_basis, right_basis, ranks):
    _, n, s = sources_field.shape
    m = data.shape[1]
    k = left_basis.shape[-1]
    groups = tiles // group
    dma = pltpu.SemaphoreType.DMA
    whole = pl.BlockSpec(memory_space=pl.ANY)
    return pl.pallas_call(
        functools.partial(plain_kernel, tiles, group),
        out_shape=(
            jax.ShapeDtypeStruct((2, m, s), F32),
            jax.ShapeDtypeStruct((2, n, s), F32),
        ),
        in_specs=[pl.BlockSpec(memory_space=pltpu.SMEM)] + [whole] * 4,
        out_specs=(whole, whole),
        scratch_shapes=[
            pltpu.VMEM((2, n, s), F32),
            pltpu.VMEM((2, m, s), F32),
            pltpu.VMEM((2, tiles, m, k), F32),
            pltpu.VMEM((2, tiles, n, k), F32),
            pltpu.VMEM((2, tiles, s, k), F32),
            pltpu.VMEM((2, 2, tiles, s // 4, k), F32),
            pltpu.VMEM((2, 2, 2, tiles, s // 4, k), F32),
            pltpu.VMEM((2, 2, tiles, s, k), F32),
            pltpu.VMEM((2, 2 * s, n), BF16),
            pltpu.VMEM((2, 2 * s, m), BF16),
            pltpu.VMEM((m, 2 * s), F32),
            pltpu.VMEM((n, 2 * s), F32),
            pltpu.VMEM((2, n, s), F32),
            dma, dma, dma((groups,)), dma, dma((2,)), dma((2,)),
            dma((2, 2)), dma((2, 2)), dma((2,)), dma((2, 2)), dma((2, 2)),
            dma((2, 2, groups)), dma((2, 2, groups)), dma((2, groups)),
            dma((2, 2, groups)), dma((2, 2, groups)),
        ],
        compiler_params=pltpu.CompilerParams(
            collective_id=0, has_side_effects=True, vmem_limit_bytes=60 * 1024 * 1024
        ),
        name="tlr_plain",
    )(ranks, sources_field, data, left_basis, right_basis)


def packed_kernel(
    tiles, packs, group, ranks, x_any, d_any, u_any, v_any, res_any, grad_any,
    x, d, u, v, ucat, vcat, part, r1, r2, aout, ain00, ain01, ain10, ain11, z, xt, rt, acc_u, acc_v,
    off, tile_of, x_sem, d_sem, v_sem, u_sem, out_sem, self_sem,
    rs1_send, rs2_send, a2a_send, ag1_send, ag2_send,
    rs1_recv, rs2_recv, a2a_recv, ag1_recv, ag2_recv,
):
    c = lax.axis_index("col")
    r = lax.axis_index("row")
    thick, kmax = part.shape[-2:]
    level = kmax // 4
    s = part.shape[0] * 4 * thick
    groups = packs // group
    units = 2 * groups
    right, left = (c, lax.rem(r + 1, 4)), (c, lax.rem(r + 3, 4))
    q_right, q_left, q_far = lax.rem(r + 1, 4), lax.rem(r + 3, 4), lax.rem(r + 2, 4)
    ain = ((ain00, ain01), (ain10, ain11))

    def ahead(t):
        return lax.rem(c + t, tiles)

    def behind(t):
        return lax.rem(c + tiles - t, tiles)

    barrier = pltpu.get_barrier_semaphore()

    def greet(t, _):
        pl.semaphore_signal(barrier, inc=1, device_id=(ahead(t), r), device_id_type=MESH)
        return 0

    copy_x = pltpu.make_async_copy(x_any, x, x_sem)
    copy_x.start()

    def fetch_v(t, _):
        pltpu.make_async_copy(v_any.at[:, ahead(t)], v.at[:, t], v_sem.at[t]).start()
        return 0

    lax.fori_loop(0, tiles, fetch_v, 0)
    lax.fori_loop(1, tiles, greet, 0)
    pl.semaphore_signal(barrier, inc=1, device_id=right, device_id_type=MESH)
    pl.semaphore_signal(barrier, inc=1, device_id=left, device_id_type=MESH)

    def fetch_u(t, _):
        pltpu.make_async_copy(u_any.at[:, behind(t)], u.at[:, t], u_sem).start()
        return 0

    copy_d = pltpu.make_async_copy(d_any, d, d_sem)

    def tabulate(k, rank_of):
        off[k, 0] = 0

        def add(t, _):
            off[k, t + 1] = off[k, t] + rank_of(t) // level
            return 0

        lax.fori_loop(0, tiles, add, 0)

        def place(b, t):
            t = jnp.minimum(t + (b >= off[k, t + 1]).astype(jnp.int32), tiles - 1)
            tile_of[k, b] = t
            return t

        lax.fori_loop(0, 4 * packs, place, 0)

    def lanes(rows):
        return lax.broadcasted_iota(jnp.int32, (rows, kmax), 1)

    def in_place(k, t, run):
        return pltpu.roll(run, (off[k, t] & 3) * level, 1)

    def packed(k, p, load):
        out = None
        for m in range(4):
            run = load(tile_of[k, 4 * p + m])
            out = run if m == 0 else jnp.where(lanes(run.shape[0]) >= m * level, run, out)
        return out

    def shift_basis(k, basis, t):
        for h in range(2):
            basis[h, t] = in_place(k, t, basis[h, t])

    def pack_basis(k, basis, cat, p):
        for h in range(2):
            hi, lo = halves(packed(k, p, lambda t: basis[h, t]))
            cat[0, p, :, h * kmax : (h + 1) * kmax] = hi
            cat[1, p, :, h * kmax : (h + 1) * kmax] = lo

    def span(g):
        return pl.ds(g * group, group)

    def wait_for(ref, sem):
        pltpu.make_async_copy(ref, ref, sem).wait()

    def send(src, dst, send_sem, recv_sem, to):
        pltpu.make_async_remote_copy(
            src_ref=src, dst_ref=dst, send_sem=send_sem, recv_sem=recv_sem,
            device_id=to, device_id_type=MESH,
        ).start()

    def phase(ph, makes, made_k, owner_of, spreads, spread_k):
        def halved(e):
            return lax.div(e, groups), lax.rem(e, groups)

        def each(g, f):
            def one(j, _):
                f(g * group + j)
                return 0

            lax.fori_loop(0, group, one, 0, unroll=group)

        def produce(g):
            def one(p):
                pack_basis(0, v, vcat, p)
                y = dot3((xt[0], xt[1]), (makes[0, p], makes[1, p]), ((1,), (0,)))
                part[:, 0, :, p] = (y[:s, :kmax] + y[s:, kmax:]).reshape(2, 4, thick, kmax)
                part[:, 1, :, p] = (y[s:, :kmax] - y[:s, kmax:]).reshape(2, 4, thick, kmax)

            each(g, one)

        def produce_half(f, g):
            n = s // 2

            def one(p):
                y = dot3((rt[f, 0], rt[f, 1]), (makes[0, p], makes[1, p]), ((1,), (0,)))
                part[f, 0, :, p] = (y[:n, :kmax] + y[n:, kmax:]).reshape(4, thick, kmax)
                part[f, 1, :, p] = (y[n:, :kmax] - y[:n, kmax:]).reshape(4, thick, kmax)

            each(g, one)

        def sums_sent(f):
            for h, q in ((0, q_right), (1, q_left)):
                wait_for(part.at[f, h, q_far], rs1_send.at[ph, f, h])
                wait_for(part.at[f, :, q], rs2_send.at[ph, f, h])

        def dealt(f):
            wait_for(aout.at[f, pl.ds(1, tiles - 1)], a2a_send.at[ph, f])

        def gathered():
            for h, q in ((0, q_left), (1, q_right)):
                wait_for(z.at[ph, :, :, r], ag1_send.at[ph, h])
                wait_for(z.at[ph, :, h, q], ag2_send.at[ph, h])

        def rs1(e):
            f, g = halved(e)
            send(part.at[f, 0, q_far, span(g)], r1.at[ph, f, 0, span(g)],
                 rs1_send.at[ph, f, 0], rs1_recv.at[ph, 0, e], right)
            send(part.at[f, 1, q_far, span(g)], r1.at[ph, f, 1, span(g)],
                 rs1_send.at[ph, f, 1], rs1_recv.at[ph, 1, e], left)

        def rs2(e):
            f, g = halved(e)
            for h, q, to in ((0, q_right, right), (1, q_left, left)):
                wait_for(r1.at[ph, f, h, span(g)], rs1_recv.at[ph, h, e])
                part[f, h, q, span(g)] = part[f, h, q, span(g)] + r1[ph, f, h, span(g)]
                send(part.at[f, :, q, span(g)], r2.at[ph, f, h, :, span(g)],
                     rs2_send.at[ph, f, h], rs2_recv.at[ph, h, e], to)

        def settle(e):
            f, g = halved(e)
            for h in range(2):
                wait_for(r2.at[ph, f, h, :, span(g)], rs2_recv.at[ph, h, e])
            for h in range(2):
                part[f, h, r, span(g)] = part[f, h, r, span(g)] + (
                    r2[ph, f, 0, h, span(g)] + r2[ph, f, 1, h, span(g)]
                )

        def deal(f):
            def unpack(t, _):
                start = off[made_k, t]
                p, m = start >> 2, start & 3
                after = jnp.minimum(p + 1, packs - 1)
                for h in range(2):
                    both = jnp.where(
                        lanes(thick) >= m * level, part[f, h, r, p], part[f, h, r, after]
                    )
                    aout[f, t, h] = pltpu.roll(both, ((4 - m) & 3) * level, 1)
                return 0

            lax.fori_loop(0, tiles, unpack, 0, unroll=UNROLL)
            pltpu.make_async_copy(aout.at[f, 0], ain[ph][f].at[0], self_sem.at[ph, f]).start()

            def one(j, _):
                t = lax.rem(j * STRIDE, tiles)
                send(aout.at[f, t], ain[ph][f].at[t], a2a_send.at[ph, f],
                     a2a_recv.at[ph, f], (owner_of(t), r))
                return 0

            lax.fori_loop(1, tiles, one, 0)

        def gather(f):
            got = ain[ph][f]
            wait_for(got.at[0], self_sem.at[ph, f])
            wait_for(got.at[pl.ds(1, tiles - 1)], a2a_recv.at[ph, f])
            total = off[spread_k, tiles] * level

            def one(p, _):
                kept = lanes(thick) + p * kmax < total
                for h in range(2):
                    block = packed(spread_k, p, lambda t: in_place(spread_k, t, got[t, h]))
                    z[ph, f, h, r, p] = jnp.where(kept, block, 0.0)
                return 0

            lax.fori_loop(0, packs, one, 0, unroll=group)

        def ag1(e):
            f, g = halved(e)
            own = z.at[ph, f, :, r, span(g)]
            send(own, own, ag1_send.at[ph, 0], ag1_recv.at[ph, 0, e], right)
            send(own, own, ag1_send.at[ph, 1], ag1_recv.at[ph, 1, e], left)

        def ag2(e):
            f, g = halved(e)
            for h, q, to in ((0, q_left, right), (1, q_right, left)):
                wait_for(z.at[ph, f, :, q, span(g)], ag1_recv.at[ph, h, e])
                passed = z.at[ph, f, h, q, span(g)]
                send(passed, passed, ag2_send.at[ph, h], ag2_recv.at[ph, h, e], to)

        def arrived(f, g):
            for h in range(2):
                wait_for(z.at[ph, f, h, q_far, span(g)], ag2_recv.at[ph, h, f * groups + g])

        def spread(g, coeffs):
            wide, tall = [], []
            for j in range(group):
                p = g * group + j
                (ah, al), (bh, bl) = (halves(coeffs(h, p)) for h in range(2))

                def square(a, b):
                    return jnp.concatenate(
                        [jnp.concatenate([a, -b], axis=1), jnp.concatenate([b, a], axis=1)], axis=0
                    )

                high, low = square(ah, bh), square(al, bl)
                wide += [spreads[0, p], spreads[0, p], spreads[1, p]]
                tall += [high, low, high]
            return lax.dot_general(
                jnp.concatenate(wide, axis=1), jnp.concatenate(tall, axis=1),
                (((1,), (1,)), ((), ())), preferred_element_type=F32,
            )

        def consume(g):
            for f in range(2):
                arrived(f, g)
            acc_v[...] += spread(g, lambda h, p: z[ph, :, h, :, p].reshape(s, kmax))

        def consume_half(f, g):
            arrived(f, g)
            acc_u[f] += spread(g, lambda h, p: z[ph, f, h, :, p].reshape(s // 2, kmax))

        return types.SimpleNamespace(**locals())

    fwd = phase(0, vcat, 0, ahead, ucat, 1)
    adj = phase(1, ucat, 1, behind, vcat, 0)

    def subtract(f):
        n = s // 2
        given = jnp.concatenate([d[h, :, f * n : (f + 1) * n] for h in range(2)], axis=1)
        rest = acc_u[f] - given
        hi, lo = halves(rest.T)
        rt[f, 0] = hi
        rt[f, 1] = lo
        for h in range(2):
            d[h, :, f * n : (f + 1) * n] = rest[:, h * n : (h + 1) * n]

    sum1, sum2, own = (2, groups + 2), (4, groups + 4), (groups + 7, 2 * groups + 7)
    passes, used = (own[0] + 2, own[1] + 2), (own[0] + 4, own[1] + 4)
    second = used[0] + groups
    chunk = -(-tiles // 4)

    def step(it, _):
        def at(first, count, f, base=0):
            @pl.when((it >= first) & (it < first + count))
            def _():
                f(it - first + base)

        def both(first, f):
            at(first[0], groups, f)
            at(first[1], groups, f, groups)

        def once(when, f, *given):
            at(when, 1, lambda _: f(*given))

        def later(pair):
            return tuple(first + second for first in pair)

        at(0, groups, fwd.produce)
        at(0, units, fwd.rs1)
        once(own[0], fwd.gather, 0)
        once(own[1], fwd.gather, 1)
        both(own, fwd.ag1)
        both(sum1, fwd.rs2)
        both(passes, fwd.ag2)
        once(groups, tabulate, 1, lambda t: ranks[c, behind(t)])
        once(groups, wait_for, u, u_sem)

        def shift(j):
            def one(t, _):
                shift_basis(1, u, t)
                return 0

            lax.fori_loop(j * chunk, jnp.minimum((j + 1) * chunk, tiles), one, 0)

        at(groups, 4, shift)
        at(groups + 4, groups, lambda g: fwd.each(g, functools.partial(pack_basis, 1, u, ucat)))
        both(sum2, fwd.settle)
        for f in range(2):
            once(sum2[f] + groups - 1, fwd.deal, f)
        once(used[0], copy_d.wait)
        for f in range(2):
            at(used[f], groups, functools.partial(fwd.consume_half, f))
            once(used[f] + groups - 1, subtract, f)

        for f in range(2):
            once(second + f * groups, fwd.sums_sent, f)
            at(second + f * groups, groups, functools.partial(adj.produce_half, f))
        at(second, units, adj.rs1)
        once(second + own[0], adj.gather, 0)
        once(second + own[1], adj.gather, 1)
        both(later(own), adj.ag1)
        both(later(sum1), adj.rs2)
        both(later(passes), adj.ag2)
        both(later(sum2), adj.settle)
        for f in range(2):
            once(second + sum2[f] + groups - 1, fwd.dealt, f)
            once(second + sum2[f] + groups - 1, adj.deal, f)
        once(second + 2 * groups, lambda: copy_res.start())
        at(second + used[1], groups, adj.consume)
        return 0

    copy_res = pltpu.make_async_copy(d, res_any, out_sem.at[0])
    acc_u[...] = jnp.zeros_like(acc_u)
    acc_v[...] = jnp.zeros_like(acc_v)
    tabulate(0, lambda t: ranks[ahead(t), c])
    copy_x.wait()
    for p in range(2):
        hi, lo = halves(x[p].T)
        xt[0, p * s : (p + 1) * s] = hi
        xt[1, p * s : (p + 1) * s] = lo

    def settle_v(t, _):
        wait_for(v.at[:, t], v_sem.at[t])
        return 0

    lax.fori_loop(0, tiles, settle_v, 0)

    def shift_v(t, _):
        shift_basis(0, v, t)
        return 0

    lax.fori_loop(0, tiles, shift_v, 0, unroll=UNROLL)
    lax.fori_loop(0, tiles, fetch_u, 0)
    copy_d.start()
    pl.semaphore_wait(barrier, tiles + 1)
    lax.fori_loop(0, second + used[1] + groups, step, 0)

    for p in range(2):
        x[p] = acc_v[:, p * s : (p + 1) * s]
    copy_grad = pltpu.make_async_copy(x, grad_any, out_sem.at[1])
    copy_grad.start()
    fwd.gathered()
    adj.gathered()
    for f in range(2):
        adj.sums_sent(f)
        adj.dealt(f)
    copy_res.wait()
    copy_grad.wait()


def packed_step(tiles, packs, group, collective_id, sources_field, data, left_basis, right_basis, ranks):
    _, n, s = sources_field.shape
    m = data.shape[1]
    k = left_basis.shape[-1]
    units = 2 * packs // group
    thick = s // 8
    dma = pltpu.SemaphoreType.DMA
    whole = pl.BlockSpec(memory_space=pl.ANY)
    dealt = pltpu.VMEM((tiles, 2, thick, k), F32)
    return pl.pallas_call(
        functools.partial(packed_kernel, tiles, packs, group),
        out_shape=(
            jax.ShapeDtypeStruct((2, m, s), F32),
            jax.ShapeDtypeStruct((2, n, s), F32),
        ),
        in_specs=[pl.BlockSpec(memory_space=pltpu.SMEM)] + [whole] * 4,
        out_specs=(whole, whole),
        scratch_shapes=[
            pltpu.VMEM((2, n, s), F32),
            pltpu.VMEM((2, m, s), F32),
            pltpu.VMEM((2, tiles, m, k), F32),
            pltpu.VMEM((2, tiles, n, k), F32),
            pltpu.VMEM((2, packs, m, 2 * k), BF16),
            pltpu.VMEM((2, packs, n, 2 * k), BF16),
            pltpu.VMEM((2, 2, 4, packs, thick, k), F32),
            pltpu.VMEM((2, 2, 2, packs, thick, k), F32),
            pltpu.VMEM((2, 2, 2, 2, packs, thick, k), F32),
            pltpu.VMEM((2, tiles, 2, thick, k), F32),
            dealt, dealt, dealt, dealt,
            pltpu.VMEM((2, 2, 2, 4, packs, thick, k), F32),
            pltpu.VMEM((2, 2 * s, n), BF16),
            pltpu.VMEM((2, 2, s, m), BF16),
            pltpu.VMEM((2, m, s), F32),
            pltpu.VMEM((n, 2 * s), F32),
            pltpu.SMEM((2, tiles + 1), jnp.int32),
            pltpu.SMEM((2, 4 * packs), jnp.int32),
            dma, dma, dma((tiles,)), dma, dma((2,)), dma((2, 2)),
            dma((2, 2, 2)), dma((2, 2, 2)), dma((2, 2)), dma((2, 2)), dma((2, 2)),
            dma((2, 2, units)), dma((2, 2, units)), dma((2, 2)),
            dma((2, 2, units)), dma((2, 2, units)),
        ],
        compiler_params=pltpu.CompilerParams(
            collective_id=collective_id, has_side_effects=True, vmem_limit_bytes=60 * 1024 * 1024
        ),
        name="tlr_packed",
    )(ranks, sources_field, data, left_basis, right_basis)


def on_device(tiles, group, sizes, *args):
    runs = args[4] // (args[2].shape[-1] // 4)
    most = jnp.stack([runs, runs.T]).sum(1).max()
    choice = sum((most > 4 * packs).astype(jnp.int32) for packs, _ in sizes)
    forms = [
        functools.partial(packed_step, tiles, packs, pack_group, 1 + i)
        for i, (packs, pack_group) in enumerate(sizes)
    ]
    return lax.switch(choice, forms + [functools.partial(plain_step, tiles, group)], *args)


def solution(mesh):
    tiles = mesh.shape["col"]
    wide = tiles % GROUP == 0 and tiles > 2 * GROUP
    sizes = SIZES if wide else ((tiles, 1),)
    placed = P(None, ("col", "row"), None)
    bases = P(None, None, ("col", "row"), None)
    return jax.shard_map(
        functools.partial(on_device, tiles, GROUP if wide else 1, sizes),
        mesh=mesh,
        in_specs=(placed, placed, bases, bases, P()),
        out_specs=(placed, placed),
        check_vma=False,
    )
```

```python
import functools
import types

import jax
import jax.numpy as jnp
from jax import lax
from jax.experimental import pallas as pl
from jax.experimental.pallas import tpu as pltpu
from jax.sharding import PartitionSpec as P

MESH = pl.DeviceIdType.MESH
F32 = jnp.float32
BF16 = jnp.bfloat16
GROUP = 4
SIZES = ((24, 6), (25, 5))
UNROLL = 8
STRIDE = 11


def halves(a):
    hi = a.astype(BF16)
    return hi, (a - hi.astype(F32)).astype(BF16)


def dot3(a, b, contract):
    def dot(x, y):
        return lax.dot_general(x, y, (contract, ((), ())), preferred_element_type=F32)

    (ah, al), (bh, bl) = a, b
    return dot(ah, bh) + (dot(ah, bl) + dot(al, bh))


def plain_kernel(
    tiles, group, ranks, x_any, d_any, u_any, v_any, res_any, grad_any,
    x, d, u, v, part, r1, r2, z, xt, rt, acc_u, acc_v, grad,
    x_sem, d_sem, v_sem, u_sem, out_sem, self_sem,
    rs1_send, rs2_send, a2a_send, ag1_send, ag2_send,
    rs1_recv, rs2_recv, a2a_recv, ag1_recv, ag2_recv,
):
    c = lax.axis_index("col")
    r = lax.axis_index("row")
    s = part.shape[-2]
    quarter = s // 4
    groups = tiles // group
    right, left = (c, lax.rem(r + 1, 4)), (c, lax.rem(r + 3, 4))

    barrier = pltpu.get_barrier_semaphore()

    def greet(t, _):
        peer = (lax.rem(c + t, tiles), r)
        pl.semaphore_signal(barrier, inc=1, device_id=peer, device_id_type=MESH)
        return 0

    lax.fori_loop(1, tiles, greet, 0)
    pl.semaphore_signal(barrier, inc=1, device_id=right, device_id_type=MESH)
    pl.semaphore_signal(barrier, inc=1, device_id=left, device_id_type=MESH)

    copy_x = pltpu.make_async_copy(x_any, x, x_sem)
    copy_x.start()

    def fetch_v(t, _):
        pltpu.make_async_copy(
            v_any.at[:, lax.rem(c + t, tiles)], v.at[:, t], v_sem.at[t // group]
        ).start()
        return 0

    lax.fori_loop(0, tiles, fetch_v, 0)

    def fetch_u(t, _):
        pltpu.make_async_copy(u_any.at[:, lax.rem(c + t, tiles)], u.at[:, t], u_sem).start()
        return 0

    lax.fori_loop(0, tiles, fetch_u, 0)
    copy_d = pltpu.make_async_copy(d_any, d, d_sem)
    copy_d.start()

    def rows(q):
        return pl.ds(pl.multiple_of(q * quarter, quarter), quarter)

    def span(g):
        return pl.ds(g * group, group)

    def turned(values, dst):
        for p in range(2):
            hi, lo = halves(values[p].T)
            dst[0, p * s : (p + 1) * s] = hi
            dst[1, p * s : (p + 1) * s] = lo

    def wait_for(ref, sem):
        pltpu.make_async_copy(ref, ref, sem).wait()

    def phase(ph, made_from, lhs, rank_of, spread_by, acc):
        q_right, q_left, q_far = lax.rem(r + 1, 4), lax.rem(r + 3, 4), lax.rem(r + 2, 4)

        def send(src, dst, send_sem, recv_sem, to):
            pltpu.make_async_remote_copy(
                src_ref=src, dst_ref=dst, send_sem=send_sem, recv_sem=recv_sem,
                device_id=to, device_id_type=MESH,
            ).start()

        def produce(g):
            if ph == 0:
                wait_for(v.at[:, span(g)], v_sem.at[g])

            def one(k, _):
                t = g * group + k
                both = jnp.concatenate([made_from[0, t], made_from[1, t]], axis=1)
                y = dot3((lhs[0], lhs[1]), halves(both), ((1,), (0,)))
                kmax = y.shape[1] // 2
                level = lax.broadcasted_iota(jnp.int32, (s, kmax), 1)
                keep = level < rank_of(t)
                part[0, t] = jnp.where(keep, y[:s, :kmax] + y[s:, kmax:], 0.0)
                part[1, t] = jnp.where(keep, y[s:, :kmax] - y[:s, kmax:], 0.0)
                return 0

            lax.fori_loop(0, group, one, 0)

        def rs1(g):
            send(part.at[0, span(g), rows(q_far)], r1.at[ph, 0, span(g)],
                 rs1_send.at[ph, 0], rs1_recv.at[ph, 0, g], right)
            send(part.at[1, span(g), rows(q_far)], r1.at[ph, 1, span(g)],
                 rs1_send.at[ph, 1], rs1_recv.at[ph, 1, g], left)

        def rs2(g):
            for h, q, to in ((0, q_right, right), (1, q_left, left)):
                wait_for(r1.at[ph, h, span(g)], rs1_recv.at[ph, h, g])
                part[h, span(g), rows(q)] = part[h, span(g), rows(q)] + r1[ph, h, span(g)]
                send(part.at[:, span(g), rows(q)], r2.at[ph, h, :, span(g)],
                     rs2_send.at[ph, h], rs2_recv.at[ph, h, g], to)

        def settle(g):
            for h in range(2):
                wait_for(r2.at[ph, h, :, span(g)], rs2_recv.at[ph, h, g])
            for h in range(2):
                part[h, span(g), rows(r)] = part[h, span(g), rows(r)] + (
                    r2[ph, 0, h, span(g)] + r2[ph, 1, h, span(g)]
                )

            def one(k, _):
                t = g * group + k
                src, dst = part.at[:, t, rows(r)], z.at[ph, :, t, rows(r)]

                @pl.when(t == 0)
                def _():
                    pltpu.make_async_copy(src, dst, self_sem.at[ph]).start()

                @pl.when(t > 0)
                def _():
                    send(src, dst, a2a_send.at[ph], a2a_recv.at[ph, g], (lax.rem(c + t, tiles), r))

                return 0

            lax.fori_loop(0, group, one, 0)

        def ag1(g):
            @pl.when(g == 0)
            def _():
                wait_for(z.at[ph, :, 0, rows(r)], self_sem.at[ph])
                if group > 1:
                    wait_for(z.at[ph, :, pl.ds(1, group - 1), rows(r)], a2a_recv.at[ph, 0])

            @pl.when(g > 0)
            def _():
                wait_for(z.at[ph, :, span(g), rows(r)], a2a_recv.at[ph, g])

            own = z.at[ph, :, span(g), rows(r)]
            send(own, own, ag1_send.at[ph, 0], ag1_recv.at[ph, 0, g], right)
            send(own, own, ag1_send.at[ph, 1], ag1_recv.at[ph, 1, g], left)

        def ag2(g):
            for h, q, to in ((0, q_left, right), (1, q_right, left)):
                wait_for(z.at[ph, :, span(g), rows(q)], ag1_recv.at[ph, h, g])
                passed = z.at[ph, h, span(g), rows(q)]
                send(passed, passed, ag2_send.at[ph, h], ag2_recv.at[ph, h, g], to)

        def consume(g):
            for h in range(2):
                wait_for(z.at[ph, h, span(g), rows(q_far)], ag2_recv.at[ph, h, g])

            def one(k, _):
                t = g * group + k
                slot = lax.rem(tiles - t, tiles)
                both = jnp.concatenate([spread_by[0, slot], spread_by[1, slot]], axis=1)
                (ah, al), (bh, bl) = halves(z[ph, 0, t]), halves(z[ph, 1, t])

                def square(a, b):
                    return jnp.concatenate(
                        [jnp.concatenate([a, -b], axis=1), jnp.concatenate([b, a], axis=1)], axis=0
                    )

                acc[...] += dot3(halves(both), (square(ah, bh), square(al, bl)), ((1,), (1,)))
                return 0

            lax.fori_loop(0, group, one, 0)

        def step(it, _):
            def at(lag, f):
                g = it - lag

                @pl.when((g >= 0) & (g < groups))
                def _():
                    f(g)

            at(0, produce)
            at(0, rs1)
            at(lag, ag1)
            at(1, rs2)
            at(2, settle)
            at(lag + 1, ag2)
            if ph == 0:

                @pl.when(it == lag + 2)
                def _():
                    wait_for(u, u_sem)

            at(lag + 2, consume)
            return 0

        lag = max(groups - 2, 3)
        if ph == 0:
            copy_x.wait()
            turned(x, xt)
        acc[...] = jnp.zeros_like(acc)
        if ph == 0:
            pl.semaphore_wait(barrier, tiles + 1)
        lax.fori_loop(0, groups + lag + 2, step, 0)

        for h, q_sum, q_pass in ((0, q_right, q_left), (1, q_left, q_right)):
            wait_for(part.at[h, :, rows(q_far)], rs1_send.at[ph, h])
            wait_for(part.at[:, :, rows(q_sum)], rs2_send.at[ph, h])
            wait_for(z.at[ph, :, :, rows(r)], ag1_send.at[ph, h])
            wait_for(z.at[ph, h, :, rows(q_pass)], ag2_send.at[ph, h])
        wait_for(part.at[:, pl.ds(1, tiles - 1), rows(r)], a2a_send.at[ph])

    phase(0, v, xt, lambda t: ranks[lax.rem(c + t, tiles), c], u, acc_u)
    copy_d.wait()
    for p in range(2):
        d[p] = acc_u[:, p * s : (p + 1) * s] - d[p]
    turned(d, rt)
    copy_res = pltpu.make_async_copy(d, res_any, out_sem.at[0])
    copy_res.start()
    phase(1, u, rt, lambda t: ranks[c, lax.rem(c + t, tiles)], v, acc_v)
    for p in range(2):
        grad[p] = acc_v[:, p * s : (p + 1) * s]
    copy_grad = pltpu.make_async_copy(grad, grad_any, out_sem.at[1])
    copy_grad.start()
    copy_res.wait()
    copy_grad.wait()


def plain_step(tiles, group, sources_field, data, left_basis, right_basis, ranks):
    _, n, s = sources_field.shape
    m = data.shape[1]
    k = left_basis.shape[-1]
    groups = tiles // group
    dma = pltpu.SemaphoreType.DMA
    whole = pl.BlockSpec(memory_space=pl.ANY)
    return pl.pallas_call(
        functools.partial(plain_kernel, tiles, group),
        out_shape=(
            jax.ShapeDtypeStruct((2, m, s), F32),
            jax.ShapeDtypeStruct((2, n, s), F32),
        ),
        in_specs=[pl.BlockSpec(memory_space=pltpu.SMEM)] + [whole] * 4,
        out_specs=(whole, whole),
        scratch_shapes=[
            pltpu.VMEM((2, n, s), F32),
            pltpu.VMEM((2, m, s), F32),
            pltpu.VMEM((2, tiles, m, k), F32),
            pltpu.VMEM((2, tiles, n, k), F32),
            pltpu.VMEM((2, tiles, s, k), F32),
            pltpu.VMEM((2, 2, tiles, s // 4, k), F32),
            pltpu.VMEM((2, 2, 2, tiles, s // 4, k), F32),
            pltpu.VMEM((2, 2, tiles, s, k), F32),
            pltpu.VMEM((2, 2 * s, n), BF16),
            pltpu.VMEM((2, 2 * s, m), BF16),
            pltpu.VMEM((m, 2 * s), F32),
            pltpu.VMEM((n, 2 * s), F32),
            pltpu.VMEM((2, n, s), F32),
            dma, dma, dma((groups,)), dma, dma((2,)), dma((2,)),
            dma((2, 2)), dma((2, 2)), dma((2,)), dma((2, 2)), dma((2, 2)),
            dma((2, 2, groups)), dma((2, 2, groups)), dma((2, groups)),
            dma((2, 2, groups)), dma((2, 2, groups)),
        ],
        compiler_params=pltpu.CompilerParams(
            collective_id=0, has_side_effects=True, vmem_limit_bytes=60 * 1024 * 1024
        ),
        name="tlr_plain",
    )(ranks, sources_field, data, left_basis, right_basis)


def packed_kernel(
    tiles, packs, group, ranks, x_any, d_any, u_any, v_any, res_any, grad_any,
    x, d, u, v, ucat, vcat, part, r1, r2, aout, ain00, ain01, ain10, ain11, z, xt, rt, acc_u, acc_v,
    off, tile_of, x_sem, d_sem, v_sem, u_sem, out_sem, self_sem,
    rs1_send, rs2_send, a2a_send, ag1_send, ag2_send,
    rs1_recv, rs2_recv, a2a_recv, ag1_recv, ag2_recv,
):
    c = lax.axis_index("col")
    r = lax.axis_index("row")
    thick, kmax = part.shape[-2:]
    level = kmax // 4
    s = part.shape[0] * 4 * thick
    groups = packs // group
    units = 2 * groups
    right, left = (c, lax.rem(r + 1, 4)), (c, lax.rem(r + 3, 4))
    q_right, q_left, q_far = lax.rem(r + 1, 4), lax.rem(r + 3, 4), lax.rem(r + 2, 4)
    ain = ((ain00, ain01), (ain10, ain11))

    def ahead(t):
        return lax.rem(c + t, tiles)

    def behind(t):
        return lax.rem(c + tiles - t, tiles)

    barrier = pltpu.get_barrier_semaphore()

    def greet(t, _):
        pl.semaphore_signal(barrier, inc=1, device_id=(ahead(t), r), device_id_type=MESH)
        return 0

    copy_x = pltpu.make_async_copy(x_any, x, x_sem)
    copy_x.start()

    def fetch_v(t, _):
        pltpu.make_async_copy(v_any.at[:, ahead(t)], v.at[:, t], v_sem.at[t]).start()
        return 0

    lax.fori_loop(0, tiles, fetch_v, 0)
    lax.fori_loop(1, tiles, greet, 0)
    pl.semaphore_signal(barrier, inc=1, device_id=right, device_id_type=MESH)
    pl.semaphore_signal(barrier, inc=1, device_id=left, device_id_type=MESH)

    def fetch_u(t, _):
        pltpu.make_async_copy(u_any.at[:, behind(t)], u.at[:, t], u_sem).start()
        return 0

    copy_d = pltpu.make_async_copy(d_any, d, d_sem)

    def tabulate(k, rank_of):
        off[k, 0] = 0

        def add(t, _):
            off[k, t + 1] = off[k, t] + rank_of(t) // level
            return 0

        lax.fori_loop(0, tiles, add, 0)

        def place(b, t):
            t = jnp.minimum(t + (b >= off[k, t + 1]).astype(jnp.int32), tiles - 1)
            tile_of[k, b] = t
            return t

        lax.fori_loop(0, 4 * packs, place, 0)

    def lanes(rows):
        return lax.broadcasted_iota(jnp.int32, (rows, kmax), 1)

    def in_place(k, t, run):
        return pltpu.roll(run, (off[k, t] & 3) * level, 1)

    def packed(k, p, load):
        out = None
        for m in range(4):
            run = load(tile_of[k, 4 * p + m])
            out = run if m == 0 else jnp.where(lanes(run.shape[0]) >= m * level, run, out)
        return out

    def shift_basis(k, basis, t):
        for h in range(2):
            basis[h, t] = in_place(k, t, basis[h, t])

    def pack_basis(k, basis, cat, p):
        for h in range(2):
            hi, lo = halves(packed(k, p, lambda t: basis[h, t]))
            cat[0, p, :, h * kmax : (h + 1) * kmax] = hi
            cat[1, p, :, h * kmax : (h + 1) * kmax] = lo

    def span(g):
        return pl.ds(g * group, group)

    def wait_for(ref, sem):
        pltpu.make_async_copy(ref, ref, sem).wait()

    def send(src, dst, send_sem, recv_sem, to):
        pltpu.make_async_remote_copy(
            src_ref=src, dst_ref=dst, send_sem=send_sem, recv_sem=recv_sem,
            device_id=to, device_id_type=MESH,
        ).start()

    def phase(ph, makes, made_k, owner_of, spreads, spread_k):
        def halved(e):
            return lax.div(e, groups), lax.rem(e, groups)

        def each(g, f):
            def one(j, _):
                f(g * group + j)
                return 0

            lax.fori_loop(0, group, one, 0, unroll=group)

        def produce(g):
            def one(p):
                pack_basis(0, v, vcat, p)
                y = dot3((xt[0], xt[1]), (makes[0, p], makes[1, p]), ((1,), (0,)))
                part[:, 0, :, p] = (y[:s, :kmax] + y[s:, kmax:]).reshape(2, 4, thick, kmax)
                part[:, 1, :, p] = (y[s:, :kmax] - y[:s, kmax:]).reshape(2, 4, thick, kmax)

            each(g, one)

        def produce_half(f, g):
            n = s // 2

            def one(p):
                y = dot3((rt[f, 0], rt[f, 1]), (makes[0, p], makes[1, p]), ((1,), (0,)))
                part[f, 0, :, p] = (y[:n, :kmax] + y[n:, kmax:]).reshape(4, thick, kmax)
                part[f, 1, :, p] = (y[n:, :kmax] - y[:n, kmax:]).reshape(4, thick, kmax)

            each(g, one)

        def sums_sent(f):
            for h, q in ((0, q_right), (1, q_left)):
                wait_for(part.at[f, h, q_far], rs1_send.at[ph, f, h])
                wait_for(part.at[f, :, q], rs2_send.at[ph, f, h])

        def dealt(f):
            wait_for(aout.at[f, pl.ds(1, tiles - 1)], a2a_send.at[ph, f])

        def gathered():
            for h, q in ((0, q_left), (1, q_right)):
                wait_for(z.at[ph, :, :, r], ag1_send.at[ph, h])
                wait_for(z.at[ph, :, h, q], ag2_send.at[ph, h])

        def rs1(e):
            f, g = halved(e)
            send(part.at[f, 0, q_far, span(g)], r1.at[ph, f, 0, span(g)],
                 rs1_send.at[ph, f, 0], rs1_recv.at[ph, 0, e], right)
            send(part.at[f, 1, q_far, span(g)], r1.at[ph, f, 1, span(g)],
                 rs1_send.at[ph, f, 1], rs1_recv.at[ph, 1, e], left)

        def rs2(e):
            f, g = halved(e)
            for h, q, to in ((0, q_right, right), (1, q_left, left)):
                wait_for(r1.at[ph, f, h, span(g)], rs1_recv.at[ph, h, e])
                part[f, h, q, span(g)] = part[f, h, q, span(g)] + r1[ph, f, h, span(g)]
                send(part.at[f, :, q, span(g)], r2.at[ph, f, h, :, span(g)],
                     rs2_send.at[ph, f, h], rs2_recv.at[ph, h, e], to)

        def settle(e):
            f, g = halved(e)
            for h in range(2):
                wait_for(r2.at[ph, f, h, :, span(g)], rs2_recv.at[ph, h, e])
            for h in range(2):
                part[f, h, r, span(g)] = part[f, h, r, span(g)] + (
                    r2[ph, f, 0, h, span(g)] + r2[ph, f, 1, h, span(g)]
                )

        def deal(f):
            def unpack(t, _):
                start = off[made_k, t]
                p, m = start >> 2, start & 3
                after = jnp.minimum(p + 1, packs - 1)
                for h in range(2):
                    both = jnp.where(
                        lanes(thick) >= m * level, part[f, h, r, p], part[f, h, r, after]
                    )
                    aout[f, t, h] = pltpu.roll(both, ((4 - m) & 3) * level, 1)
                return 0

            lax.fori_loop(0, tiles, unpack, 0, unroll=UNROLL)
            pltpu.make_async_copy(aout.at[f, 0], ain[ph][f].at[0], self_sem.at[ph, f]).start()

            def one(j, _):
                t = lax.rem(j * STRIDE, tiles)
                send(aout.at[f, t], ain[ph][f].at[t], a2a_send.at[ph, f],
                     a2a_recv.at[ph, f], (owner_of(t), r))
                return 0

            lax.fori_loop(1, tiles, one, 0)

        def gather(f):
            got = ain[ph][f]
            wait_for(got.at[0], self_sem.at[ph, f])
            wait_for(got.at[pl.ds(1, tiles - 1)], a2a_recv.at[ph, f])
            total = off[spread_k, tiles] * level

            def one(p, _):
                kept = lanes(thick) + p * kmax < total
                for h in range(2):
                    block = packed(spread_k, p, lambda t: in_place(spread_k, t, got[t, h]))
                    z[ph, f, h, r, p] = jnp.where(kept, block, 0.0)
                return 0

            lax.fori_loop(0, packs, one, 0, unroll=group)

        def ag1(e):
            f, g = halved(e)
            own = z.at[ph, f, :, r, span(g)]
            send(own, own, ag1_send.at[ph, 0], ag1_recv.at[ph, 0, e], right)
            send(own, own, ag1_send.at[ph, 1], ag1_recv.at[ph, 1, e], left)

        def ag2(e):
            f, g = halved(e)
            for h, q, to in ((0, q_left, right), (1, q_right, left)):
                wait_for(z.at[ph, f, :, q, span(g)], ag1_recv.at[ph, h, e])
                passed = z.at[ph, f, h, q, span(g)]
                send(passed, passed, ag2_send.at[ph, h], ag2_recv.at[ph, h, e], to)

        def arrived(f, g):
            for h in range(2):
                wait_for(z.at[ph, f, h, q_far, span(g)], ag2_recv.at[ph, h, f * groups + g])

        def spread(g, coeffs):
            wide, tall = [], []
            for j in range(group):
                p = g * group + j
                (ah, al), (bh, bl) = (halves(coeffs(h, p)) for h in range(2))

                def square(a, b):
                    return jnp.concatenate(
                        [jnp.concatenate([a, -b], axis=1), jnp.concatenate([b, a], axis=1)], axis=0
                    )

                high, low = square(ah, bh), square(al, bl)
                wide += [spreads[0, p], spreads[0, p], spreads[1, p]]
                tall += [high, low, high]
            return lax.dot_general(
                jnp.concatenate(wide, axis=1), jnp.concatenate(tall, axis=1),
                (((1,), (1,)), ((), ())), preferred_element_type=F32,
            )

        def consume(g):
            for f in range(2):
                arrived(f, g)
            acc_v[...] += spread(g, lambda h, p: z[ph, :, h, :, p].reshape(s, kmax))

        def consume_half(f, g):
            arrived(f, g)
            acc_u[f] += spread(g, lambda h, p: z[ph, f, h, :, p].reshape(s // 2, kmax))

        return types.SimpleNamespace(**locals())

    fwd = phase(0, vcat, 0, ahead, ucat, 1)
    adj = phase(1, ucat, 1, behind, vcat, 0)

    def subtract(f):
        n = s // 2
        given = jnp.concatenate([d[h, :, f * n : (f + 1) * n] for h in range(2)], axis=1)
        rest = acc_u[f] - given
        hi, lo = halves(rest.T)
        rt[f, 0] = hi
        rt[f, 1] = lo
        for h in range(2):
            d[h, :, f * n : (f + 1) * n] = rest[:, h * n : (h + 1) * n]

    sum1, sum2, own = (2, groups + 2), (4, groups + 4), (groups + 7, 2 * groups + 7)
    passes, used = (own[0] + 2, own[1] + 2), (own[0] + 4, own[1] + 4)
    second = used[0] + groups
    chunk = -(-tiles // 4)

    def step(it, _):
        def at(first, count, f, base=0):
            @pl.when((it >= first) & (it < first + count))
            def _():
                f(it - first + base)

        def both(first, f):
            at(first[0], groups, f)
            at(first[1], groups, f, groups)

        def once(when, f, *given):
            at(when, 1, lambda _: f(*given))

        def later(pair):
            return tuple(first + second for first in pair)

        at(0, groups, fwd.produce)
        at(0, units, fwd.rs1)
        once(own[0], fwd.gather, 0)
        once(own[1], fwd.gather, 1)
        both(own, fwd.ag1)
        both(sum1, fwd.rs2)
        both(passes, fwd.ag2)
        once(groups, tabulate, 1, lambda t: ranks[c, behind(t)])
        once(groups, wait_for, u, u_sem)

        def shift(j):
            def one(t, _):
                shift_basis(1, u, t)
                return 0

            lax.fori_loop(j * chunk, jnp.minimum((j + 1) * chunk, tiles), one, 0)

        at(groups, 4, shift)
        at(groups + 4, groups, lambda g: fwd.each(g, functools.partial(pack_basis, 1, u, ucat)))
        both(sum2, fwd.settle)
        for f in range(2):
            once(sum2[f] + groups - 1, fwd.deal, f)
        once(used[0], copy_d.wait)
        for f in range(2):
            at(used[f], groups, functools.partial(fwd.consume_half, f))
            once(used[f] + groups - 1, subtract, f)

        for f in range(2):
            once(second + f * groups, fwd.sums_sent, f)
            at(second + f * groups, groups, functools.partial(adj.produce_half, f))
        at(second, units, adj.rs1)
        once(second + own[0], adj.gather, 0)
        once(second + own[1], adj.gather, 1)
        both(later(own), adj.ag1)
        both(later(sum1), adj.rs2)
        both(later(passes), adj.ag2)
        both(later(sum2), adj.settle)
        for f in range(2):
            once(second + sum2[f] + groups - 1, fwd.dealt, f)
            once(second + sum2[f] + groups - 1, adj.deal, f)
        once(second + 2 * groups, lambda: copy_res.start())
        at(second + used[1], groups, adj.consume)
        return 0

    copy_res = pltpu.make_async_copy(d, res_any, out_sem.at[0])
    acc_u[...] = jnp.zeros_like(acc_u)
    acc_v[...] = jnp.zeros_like(acc_v)
    tabulate(0, lambda t: ranks[ahead(t), c])
    copy_x.wait()
    for p in range(2):
        hi, lo = halves(x[p].T)
        xt[0, p * s : (p + 1) * s] = hi
        xt[1, p * s : (p + 1) * s] = lo

    def settle_v(t, _):
        wait_for(v.at[:, t], v_sem.at[t])
        return 0

    lax.fori_loop(0, tiles, settle_v, 0)

    def shift_v(t, _):
        shift_basis(0, v, t)
        return 0

    lax.fori_loop(0, tiles, shift_v, 0, unroll=UNROLL)
    lax.fori_loop(0, tiles, fetch_u, 0)
    copy_d.start()
    pl.semaphore_wait(barrier, tiles + 1)
    lax.fori_loop(0, second + used[1] + groups, step, 0)

    for p in range(2):
        x[p] = acc_v[:, p * s : (p + 1) * s]
    copy_grad = pltpu.make_async_copy(x, grad_any, out_sem.at[1])
    copy_grad.start()
    fwd.gathered()
    adj.gathered()
    for f in range(2):
        adj.sums_sent(f)
        adj.dealt(f)
    copy_res.wait()
    copy_grad.wait()


def packed_step(tiles, packs, group, collective_id, sources_field, data, left_basis, right_basis, ranks):
    _, n, s = sources_field.shape
    m = data.shape[1]
    k = left_basis.shape[-1]
    units = 2 * packs // group
    thick = s // 8
    dma = pltpu.SemaphoreType.DMA
    whole = pl.BlockSpec(memory_space=pl.ANY)
    dealt = pltpu.VMEM((tiles, 2, thick, k), F32)
    return pl.pallas_call(
        functools.partial(packed_kernel, tiles, packs, group),
        out_shape=(
            jax.ShapeDtypeStruct((2, m, s), F32),
            jax.ShapeDtypeStruct((2, n, s), F32),
        ),
        in_specs=[pl.BlockSpec(memory_space=pltpu.SMEM)] + [whole] * 4,
        out_specs=(whole, whole),
        scratch_shapes=[
            pltpu.VMEM((2, n, s), F32),
            pltpu.VMEM((2, m, s), F32),
            pltpu.VMEM((2, tiles, m, k), F32),
            pltpu.VMEM((2, tiles, n, k), F32),
            pltpu.VMEM((2, packs, m, 2 * k), BF16),
            pltpu.VMEM((2, packs, n, 2 * k), BF16),
            pltpu.VMEM((2, 2, 4, packs, thick, k), F32),
            pltpu.VMEM((2, 2, 2, packs, thick, k), F32),
            pltpu.VMEM((2, 2, 2, 2, packs, thick, k), F32),
            pltpu.VMEM((2, tiles, 2, thick, k), F32),
            dealt, dealt, dealt, dealt,
            pltpu.VMEM((2, 2, 2, 4, packs, thick, k), F32),
            pltpu.VMEM((2, 2 * s, n), BF16),
            pltpu.VMEM((2, 2, s, m), BF16),
            pltpu.VMEM((2, m, s), F32),
            pltpu.VMEM((n, 2 * s), F32),
            pltpu.SMEM((2, tiles + 1), jnp.int32),
            pltpu.SMEM((2, 4 * packs), jnp.int32),
            dma, dma, dma((tiles,)), dma, dma((2,)), dma((2, 2)),
            dma((2, 2, 2)), dma((2, 2, 2)), dma((2, 2)), dma((2, 2)), dma((2, 2)),
            dma((2, 2, units)), dma((2, 2, units)), dma((2, 2)),
            dma((2, 2, units)), dma((2, 2, units)),
        ],
        compiler_params=pltpu.CompilerParams(
            collective_id=collective_id, has_side_effects=True, vmem_limit_bytes=60 * 1024 * 1024
        ),
        name="tlr_packed",
    )(ranks, sources_field, data, left_basis, right_basis)


def on_device(tiles, group, sizes, *args):
    runs = args[4] // (args[2].shape[-1] // 4)
    most = jnp.stack([runs, runs.T]).sum(1).max()
    choice = sum((most > 4 * packs).astype(jnp.int32) for packs, _ in sizes)
    forms = [
        functools.partial(packed_step, tiles, packs, pack_group, 1 + i)
        for i, (packs, pack_group) in enumerate(sizes)
    ]
    return lax.switch(choice, forms + [functools.partial(plain_step, tiles, group)], *args)


def solution(mesh):
    tiles = mesh.shape["col"]
    wide = tiles % GROUP == 0 and tiles > 2 * GROUP
    sizes = SIZES if wide else ((tiles, 1),)
    placed = P(None, ("col", "row"), None)
    bases = P(None, None, ("col", "row"), None)
    return jax.shard_map(
        functools.partial(on_device, tiles, GROUP if wide else 1, sizes),
        mesh=mesh,
        in_specs=(placed, placed, bases, bases, P()),
        out_specs=(placed, placed),
        check_vma=False,
    )
```
